512 devices in a mesh: gz: 16 (over z), gy: 32 (over x, y, core).
Axes of the slice: x: 4, y: 4, z: 16, core: 2. Of those that a mesh axis runs over, the one named last changes fastest.
Arguments:
- tracer: float32 [512, 1024, 128], P('gz', 'gy'), may hold values from 0.1 to 10
- y_speed: float32 [512, 1024, 128], P('gz', 'gy'), may hold values from -0.4 to 0.4
- z_speed: float32 [512, 1024, 128], P('gz', 'gy'), may hold values from -0.4 to 0.4
- kappa: float32 [512, 1024, 128], P('gz', 'gy'), may hold values from 0.5 to 8
Outputs:
- updated: float32 [512, 1024, 128], P('gz', 'gy')
The draws below stay inside these ranges and needn't reach their ends.
All inputs are finite; a program needn't handle non-finite values.
Results may differ from the reference program's by a relative error of at most 0.0003.
Values sent between devices are 32-bit elements; how exact they have to be, the bound alone decides.
A program may use at most 64 MiB of HBM per device.

```python
import math
import jax
import jax.numpy as jnp
from jax import lax

XW = 128
NSUB = 4
NZ = 512
NY = 1024


def smooth_wave(count, cycles, phase):
    positions = (jnp.arange(count, dtype=jnp.float32) + 0.5) / count
    return jnp.sin(2.0 * math.pi * cycles * positions + phase)


def draw_tracer(key, part):
    phase_key = jax.random.fold_in(key, 11)
    noise_key = jax.random.fold_in(key, 12)
    phases = jax.random.uniform(phase_key, (2,), jnp.float32, 0.0, 2.0 * math.pi)
    smooth = 1.9 + 0.7 * smooth_wave(NZ, 1, phases[0])[:, None, None] + 0.7 * smooth_wave(NY, 2, phases[1])[None, :, None]
    rough = jnp.exp(jax.random.uniform(noise_key, (NZ, NY, XW), jnp.float32, math.log(0.2), math.log(3.0)))
    return smooth * rough


def draw_y_speed(key, part):
    phase_key = jax.random.fold_in(key, 21)
    noise_key = jax.random.fold_in(key, 22)
    phases = jax.random.uniform(phase_key, (2,), jnp.float32, 0.0, 2.0 * math.pi)
    noise = jax.random.uniform(noise_key, (NZ, NY, XW), jnp.float32, -0.22, 0.22)
    along_y = smooth_wave(NY, 2, phases[0])[None, :, None]
    along_z = smooth_wave(NZ, 1, phases[1])[:, None, None]
    smooth = 0.12 * along_y + 0.06 * along_z
    return smooth + noise


def draw_z_speed(key, part):
    phase_key = jax.random.fold_in(key, 31)
    noise_key = jax.random.fold_in(key, 32)
    phases = jax.random.uniform(phase_key, (2,), jnp.float32, 0.0, 2.0 * math.pi)
    noise = jax.random.uniform(noise_key, (NZ, NY, XW), jnp.float32, -0.22, 0.22)
    along_z = smooth_wave(NZ, 1, phases[0])[:, None, None]
    along_y = smooth_wave(NY, 2, phases[1])[None, :, None]
    smooth = 0.12 * along_z + 0.06 * along_y
    return smooth + noise


def levels(stream_key, dims, shards, least, high):
    level = 1.0
    for axis_at, parts in shards:
        draws = jax.random.uniform(jax.random.fold_in(jax.random.fold_in(stream_key, 6), axis_at), (parts,), jnp.float32, least / len(shards), high / len(shards))
        level = level * jnp.repeat(jnp.exp(draws), dims[axis_at] // parts).reshape((-1,) + (1,) * (len(dims) - 1 - axis_at))
    return level


def setup_inputs(seed: int = 0) -> dict:
    keys = jax.random.split(jax.random.key(seed), 5)
    return {
        "tracer": draw_tracer(jax.random.fold_in(keys[4], 71), 0),
        "y_speed": draw_y_speed(jax.random.fold_in(keys[4], 71), 0),
        "z_speed": draw_z_speed(jax.random.fold_in(keys[4], 71), 0),
        "kappa": jnp.clip(jnp.exp(math.log(8.0) - 2.7725887 * jax.random.uniform(keys[3], (NZ, NY, XW), jnp.float32) ** levels(keys[3], (NZ, NY, XW), ((0, 16), (1, 32)), -0.2, 0.2)), 0.5, 8.0),
    }


rate_const = 500.0

def advect_once(tracer, y_speed, z_speed):
    face_y = 0.5 * (y_speed[:, 1:] + y_speed[:, :-1])
    flux_y = jnp.maximum(face_y, 0.0) * tracer[:, :-1] + jnp.minimum(face_y, 0.0) * tracer[:, 1:]
    diff_y = flux_y[:, 1:] - flux_y[:, :-1]
    face_z = 0.5 * (z_speed[1:] + z_speed[:-1])
    flux_z = jnp.maximum(face_z, 0.0) * tracer[:-1] + jnp.minimum(face_z, 0.0) * tracer[1:]
    diff_z = flux_z[1:] - flux_z[:-1]
    return tracer[1:-1, 1:-1] - diff_y[1:-1] - diff_z[:, 1:-1]

def edge_faces(kappa):
    inner = rate_const * 0.5 * (kappa[..., 1:] + kappa[..., :-1])
    lower = jnp.concatenate([rate_const * kappa[..., :1], inner], axis=-1)
    upper = jnp.concatenate([inner, rate_const * kappa[..., -1:]], axis=-1)
    return (lower, upper)

def line_solve(right, lower, upper):
    low_diag = (-lower).at[..., 0].set(0.0)
    up_diag = (-upper).at[..., -1].set(0.0)
    main_diag = 1.0 + lower + upper
    return lax.linalg.tridiagonal_solve(low_diag, main_diag, up_diag, right[..., None])[..., 0]

def reference(tracer, y_speed, z_speed, kappa):
    widths = ((1, 1), (1, 1), (0, 0))
    padded_y = jnp.pad(y_speed, widths)
    padded_z = jnp.pad(z_speed, widths)
    state = tracer
    for step in range(NSUB):
        state = advect_once(jnp.pad(state, widths), padded_y, padded_z)
    lower, upper = edge_faces(jnp.moveaxis(kappa, 1, 2))
    state = jnp.moveaxis(line_solve(jnp.moveaxis(state, 1, 2), lower, upper), 2, 1)
    lower, upper = edge_faces(jnp.moveaxis(kappa, 0, 2))
    state = jnp.moveaxis(line_solve(jnp.moveaxis(state, 0, 2), lower, upper), 2, 0)
    return state
```

```python
import functools

import jax
import jax.numpy as jnp
from jax import lax
from jax.experimental import pallas as pl
from jax.experimental.pallas import tpu as pltpu
from jax.sharding import PartitionSpec as P

NSUB = 4
RATE = 500.0
HALF_RATE = 250.0
B = 32
X = 128
HZ = 4
HY = 8
C = 8
MESH = pl.DeviceIdType.MESH


def low_rows():
    return lax.broadcasted_iota(jnp.int32, (8, X), 0) < 4


def swap(t):
    return pltpu.roll(t, 4, 0)


def factor(kap, first, last, a_ref, b_ref, inv_ref, lo_ref, hi_ref, tmp_ref):
    e0 = 1.0 + first * kap[0]
    b0 = 1.0 + last * kap[B - 1]
    one = jnp.ones_like(e0)
    inv_ref[0] = e0
    lo_ref[0] = one
    tmp_ref[B - 1] = b0
    hi_ref[B - 1] = one

    def step(s, carry):
        e, eb, ac, bc, kf, kb = carry
        t = B - 1 - s
        kn = kap[s]
        kp = kap[t]
        face = HALF_RATE * (kf + kn)
        a = face / (e + face)
        e = 1.0 + a * e
        ac = ac * a
        faceb = HALF_RATE * (kb + kp)
        b = faceb / (eb + faceb)
        eb = 1.0 + b * eb
        bc = bc * b
        a_ref[s] = a
        inv_ref[s] = e
        lo_ref[s] = ac
        b_ref[t] = b
        tmp_ref[t] = eb
        hi_ref[t] = bc
        return e, eb, ac, bc, kn, kp

    lax.fori_loop(1, B, step, (e0, b0, one, one, kap[0], kap[B - 1]))

    def finish(j, carry):
        inv = 1.0 / (inv_ref[j] + tmp_ref[j] - 1.0)
        inv_ref[j] = inv
        lo_ref[j] = lo_ref[j] * inv
        hi_ref[j] = hi_ref[j] * inv
        return carry

    lax.fori_loop(0, B, finish, 0)


def put_pair(dst, row, first, second):
    low = low_rows()
    for q in range(4):
        f = first[8 * q : 8 * q + 8]
        s = second[8 * q : 8 * q + 8]
        dst[2 * q, row : row + 8] = jnp.where(low, f, swap(s))
        dst[2 * q + 1, row : row + 8] = jnp.where(low, swap(f), s)


def get_pair(src):
    low = low_rows()
    first, second = [], []
    for q in range(4):
        t0 = src[2 * q]
        t1 = src[2 * q + 1]
        first.append(jnp.where(low, t0, swap(t1)))
        second.append(jnp.where(low, swap(t0), t1))
    return jnp.concatenate(first, axis=0), jnp.concatenate(second, axis=0)


def owner_matrix(n, prm, m_ref, y_ref, rf_ref, rb_ref):
    low = low_rows()
    zero = jnp.zeros((8, X), jnp.float32)

    def face(i):
        p = prm[i - 1, 16:24]
        q = prm[i, 16:24]
        k = jnp.where(low, swap(p) + q, p + swap(q))
        return 1.0 / (HALF_RATE * k)

    y_ref[0] = zero
    y_ref[n] = zero
    r0 = prm[0, 0:8]
    rb0 = prm[n - 1, 0:8]
    rf_ref[0] = r0
    rb_ref[n - 1] = rb0
    m_ref[0] = zero
    m_ref[n - 1] = zero

    def step(s, carry):
        r, rb = carry
        z = prm[s, 0:8]
        zt = prm[s, 8:16]
        t = zt / (r + face(s) + swap(z))
        r = z - zt * t
        rf_ref[s] = r
        i = n - 1 - s
        zb = prm[i, 0:8]
        ztb = prm[i, 8:16]
        tb = ztb / (rb + face(i + 1) + swap(zb))
        rb = zb - ztb * tb
        rb_ref[i] = rb
        m_ref[s] = jnp.where(low, m_ref[s], t)
        m_ref[i] = jnp.where(low, tb, m_ref[i])
        return r, rb

    def clear(s, carry):
        m_ref[s] = zero
        return carry

    lax.fori_loop(0, n, clear, 0)
    lax.fori_loop(1, n, step, (r0, rb0))

    def admit(i, carry):
        y_ref[i] = 1.0 / (swap(rf_ref[i - 1]) + face(i) + rb_ref[i])
        return carry

    lax.fori_loop(1, n, admit, 0)


def owner_scan(n, g_ref, m_ref, u_ref, v_ref):
    zero = jnp.zeros((8, X), jnp.float32)
    u_ref[0] = zero
    v_ref[n] = zero

    def step(s, carry):
        u, v = carry
        g = g_ref[s]
        m = m_ref[s]
        u = g - m * swap(g) + m * u
        u_ref[s + 1] = u
        i = n - 1 - s
        gb = g_ref[i]
        mb = m_ref[i]
        v = gb - mb * swap(gb) + mb * v
        v_ref[i] = v
        return u, v

    lax.fori_loop(0, n, step, (zero, zero))


def owner_result(b, u_ref, v_ref, y_ref):
    low = low_rows()
    here = (swap(u_ref[b]) - v_ref[b]) * y_ref[b]
    after = (swap(u_ref[b + 1]) - v_ref[b + 1]) * y_ref[b + 1]
    return jnp.where(low, here, -swap(after))


def local_scan(r_ref, a_ref, b_ref, f_ref, g_ref, inv_ref):
    r0 = r_ref[0]
    rb0 = r_ref[B - 1]
    f_ref[0] = r0
    g_ref[B - 1] = jnp.zeros_like(r0)

    def step(s, carry):
        f, g = carry
        t = B - 1 - s
        f = r_ref[s] + a_ref[s] * f
        bg = b_ref[t] * g
        g = r_ref[t] + bg
        f_ref[s] = f
        g_ref[t] = bg
        return f, g

    f, g = lax.fori_loop(1, B, step, (r0, rb0))
    return g * inv_ref[0], f * inv_ref[B - 1]


def kernel(nz, ny, *refs):
    (c_hbm, v_hbm, w_hbm, k_hbm, o_hbm,
     ca, cb, vv, ww, kz, ky, k0, cym, cyp, czm, czp,
     ay, by, iy, ly, hy, az, bz, iz, lz, hz, tmp, rr, ff, gg, uz, out,
     psy, psz, pry, prz, gsy, gsz, gry, grz,
     my, yy, uy, vy, mz, yz, uo, vo, rf, rb,
     rsy, rsz, rety, retz,
     lsem, hsend, hrecv, psem, grsem, rtsem) = refs
    p = lax.axis_index("gz")
    g = lax.axis_index("gy")

    def zi(k):
        return lax.rem(p + k + nz, nz)

    def yi(k):
        return lax.rem(g + k + ny, ny)

    bar = pltpu.get_barrier_semaphore()

    def greet(pz, gy):
        pl.semaphore_signal(bar, inc=1, device_id=(pz, gy), device_id_type=MESH)

    for dz in (1, -1):
        for dy in (1, -1):
            greet(zi(dz), yi(dy))
    for k in range(1, nz):
        greet(zi(k), g)
    for k in range(1, ny):
        greet(p, yi(k))

    loads = [
        pltpu.make_async_copy(k_hbm, kz, lsem.at[0]),
        pltpu.make_async_copy(c_hbm, ca.at[HZ : HZ + B, HY : HY + B], lsem.at[1]),
        pltpu.make_async_copy(v_hbm, vv.at[HZ : HZ + B, HY : HY + B], lsem.at[2]),
        pltpu.make_async_copy(w_hbm, ww.at[HZ : HZ + B, HY : HY + B], lsem.at[3]),
    ]
    for ld in loads:
        ld.start()

    pl.semaphore_wait(bar, 4 + (nz - 1) + (ny - 1))

    zsrc = {1: slice(B - HZ, B), 0: slice(0, B), -1: slice(0, HZ)}
    zdst = {1: slice(0, HZ), 0: slice(HZ, HZ + B), -1: slice(HZ + B, 2 * HZ + B)}
    ysrc = {1: slice(B - HY, B), 0: slice(0, B), -1: slice(0, HY)}
    ydst = {1: slice(0, HY), 0: slice(HY, HY + B), -1: slice(HY + B, 2 * HY + B)}
    halo = []
    for dz, dy in ((1, 0), (-1, 0), (0, 1), (0, -1), (1, 1), (1, -1), (-1, 1), (-1, -1)):
        for src, dst in ((c_hbm, ca), (v_hbm, vv), (w_hbm, ww)):
            i = len(halo)
            halo.append(pltpu.make_async_remote_copy(
                src.at[zsrc[dz], ysrc[dy]], dst.at[zdst[dz], ydst[dy]],
                hsend.at[i], hrecv.at[i],
                device_id=(zi(dz), yi(dy)), device_id_type=MESH))
    for h in halo:
        h.start()

    loads[0].wait()
    kflat = kz.reshape(B * B, X)

    def turn(j, carry):
        ky[j] = kflat[pl.ds(j, B, stride=B), :]
        return carry

    lax.fori_loop(0, B, turn, 0)
    yfirst = jnp.where(g == 0, RATE, 0.0).astype(jnp.float32)
    ylast = jnp.where(g == ny - 1, RATE, 0.0).astype(jnp.float32)
    zfirst = jnp.where(p == 0, RATE, 0.0).astype(jnp.float32)
    zlast = jnp.where(p == nz - 1, RATE, 0.0).astype(jnp.float32)

    factor(ky, yfirst, ylast, ay, by, iy, ly, hy, tmp)
    put_pair(psy, 0, ly[0], hy[B - 1])
    put_pair(psy, 8, hy[0], hy[0])
    put_pair(psy, 16, ky[0], ky[B - 1])
    pry[g] = psy[lax.rem(g, C)]

    def to_y(src, dst, sem, k):
        return pltpu.make_async_remote_copy(
            src.at[lax.rem(g + k, C)], dst.at[g], sem.at[0], sem.at[1],
            device_id=(p, yi(k)), device_id_type=MESH)

    def to_z(src, dst, sem, k):
        return pltpu.make_async_remote_copy(
            src.at[lax.rem(p + k, C)], dst.at[p], sem.at[0], sem.at[1],
            device_id=(zi(k), g), device_id_type=MESH)

    def wait_all(ref, count, sem):
        part = ref.at[pl.ds(0, count)]
        pltpu.make_async_copy(part, part, sem).wait()

    for k in range(1, ny):
        to_y(psy, pry, psem.at[0], k).start()

    factor(kz, zfirst, zlast, az, bz, iz, lz, hz, tmp)
    put_pair(psz, 0, lz[0], hz[B - 1])
    put_pair(psz, 8, hz[0], hz[0])
    put_pair(psz, 16, kz[0], kz[B - 1])
    prz[p] = psz[lax.rem(p, C)]
    for k in range(1, nz):
        to_z(psz, prz, psem.at[1], k).start()

    for ld in loads[1:]:
        ld.wait()
    for h in halo:
        h.wait_recv()

    zero3 = jnp.zeros((HZ, B + 2 * HY, X), jnp.float32)
    zero_row = jnp.zeros((HY, X), jnp.float32)

    def zero_y(at):
        def body(z, carry):
            for ref in (ca, vv, ww):
                ref[z, at : at + HY] = zero_row
            return carry

        lax.fori_loop(0, B + 2 * HZ, body, 0)

    @pl.when(p == 0)
    def _():
        for ref in (ca, vv, ww):
            ref[0:HZ] = zero3

    @pl.when(p == nz - 1)
    def _():
        for ref in (ca, vv, ww):
            ref[HZ + B : 2 * HZ + B] = zero3

    @pl.when(g == 0)
    def _():
        zero_y(0)

    @pl.when(g == ny - 1)
    def _():
        zero_y(HY + B)

    LO, N5 = 4, B + 8

    def weights(z, carry):
        vc = vv[z, LO : LO + N5]
        vm = vv[z, LO - 1 : LO - 1 + N5]
        vp = vv[z, LO + 1 : LO + 1 + N5]
        wc = ww[z, LO : LO + N5]
        wm = ww[z - 1, LO : LO + N5]
        wp = ww[z + 1, LO : LO + N5]
        fyp = 0.5 * (vc + vp)
        fym = 0.5 * (vm + vc)
        fzp = 0.5 * (wc + wp)
        fzm = 0.5 * (wm + wc)
        cyp[z] = -jnp.minimum(fyp, 0.0)
        cym[z] = jnp.maximum(fym, 0.0)
        czp[z] = -jnp.minimum(fzp, 0.0)
        czm[z] = jnp.maximum(fzm, 0.0)
        k0[z] = (1.0 - jnp.maximum(fyp, 0.0) + jnp.minimum(fym, 0.0)
                 - jnp.maximum(fzp, 0.0) + jnp.minimum(fzm, 0.0))
        return carry

    lax.fori_loop(1, B + 2 * HZ - 1, weights, 0)

    wrefs = (k0, cym, cyp, czm, czp)
    zero_w = jnp.zeros((HZ - 1, N5, X), jnp.float32)

    def zero_wy(at):
        def body(z, carry):
            for ref in wrefs:
                ref[z, at : at + 4] = jnp.zeros((4, X), jnp.float32)
            return carry

        lax.fori_loop(1, B + 2 * HZ - 1, body, 0)

    @pl.when(p == 0)
    def _():
        for ref in wrefs:
            ref[1:HZ] = zero_w

    @pl.when(p == nz - 1)
    def _():
        for ref in wrefs:
            ref[HZ + B : 2 * HZ + B - 1] = zero_w

    @pl.when(g == 0)
    def _():
        zero_wy(0)

    @pl.when(g == ny - 1)
    def _():
        zero_wy(4 + B)

    for s in range(1, NSUB + 1):
        src, dst = (ca, cb) if s % 2 == 1 else (cb, ca)

        def sub(z, carry, src=src, dst=dst):
            new = (k0[z] * src[z, LO : LO + N5]
                   + cym[z] * src[z, LO - 1 : LO - 1 + N5]
                   + cyp[z] * src[z, LO + 1 : LO + 1 + N5]
                   + czm[z] * src[z - 1, LO : LO + N5]
                   + czp[z] * src[z + 1, LO : LO + N5])
            dst[z, LO : LO + N5] = new
            return carry

        lax.fori_loop(s, B + 2 * HZ - s, sub, 0)

    cflat = ca.reshape((B + 2 * HZ) * (B + 2 * HY), X)

    def turn_r(j, carry):
        rr[j] = cflat[pl.ds(HZ * (B + 2 * HY) + HY + j, B, stride=B + 2 * HY), :]
        return carry

    lax.fori_loop(0, B, turn_r, 0)
    g0, gl = local_scan(rr, ay, by, ff, gg, iy)
    put_pair(gsy, 0, g0, gl)
    gry[g] = gsy[lax.rem(g, C)]
    for k in range(1, ny):
        to_y(gsy, gry, grsem.at[0], k).start()

    wait_all(pry, ny - 1, psem.at[0, 1])
    owner_matrix(ny, pry, my, yy, rf, rb)

    def base(j, carry):
        ff[j] = (ff[j] + gg[j]) * inv_now[j]
        return carry

    inv_now = iy
    lax.fori_loop(0, B, base, 0)

    wait_all(gry, ny - 1, grsem.at[0, 1])
    owner_scan(ny, gry, my, uy, vy)
    yc = lax.rem(g, C)
    yb = g - yc
    rety[yc] = owner_result(g, uy, vy, yy)
    for m in range(1, C):
        b = yb + lax.rem(yc + m, C)
        rsy[m] = owner_result(b, uy, vy, yy)
        pltpu.make_async_remote_copy(
            rsy.at[m], rety.at[yc], rtsem.at[0, 0], rtsem.at[0, 1],
            device_id=(p, b), device_id_type=MESH).start()

    wait_all(prz, nz - 1, psem.at[1, 1])
    owner_matrix(nz, prz, mz, yz, rf, rb)

    wait_all(rety, C - 1, rtsem.at[0, 1])
    flo, fhi = get_pair(rety)
    uflat = uz.reshape(B * B, X)

    def end_y(j, carry):
        uflat[pl.ds(j, B, stride=B), :] = ff[j] + flo * ly[j] + fhi * hy[j]
        return carry

    lax.fori_loop(0, B, end_y, 0)

    g0, gl = local_scan(uz, az, bz, ff, gg, iz)
    put_pair(gsz, 0, g0, gl)
    grz[p] = gsz[lax.rem(p, C)]
    for k in range(1, nz):
        to_z(gsz, grz, grsem.at[1], k).start()
    inv_now = iz

    def base_z(j, carry):
        ff[j] = (ff[j] + gg[j]) * iz[j]
        return carry

    lax.fori_loop(0, B, base_z, 0)
    wait_all(grz, nz - 1, grsem.at[1, 1])
    owner_scan(nz, grz, mz, uo, vo)
    zc = lax.rem(p, C)
    retz[zc] = owner_result(p, uo, vo, yz)
    others = [o for o in range(-(C // 2), C // 2) if o != 0]
    for m, o in enumerate(others):
        b = zi(o)
        rsz[m] = owner_result(b, uo, vo, yz)
        pltpu.make_async_remote_copy(
            rsz.at[m], retz.at[zc], rtsem.at[1, 0], rtsem.at[1, 1],
            device_id=(b, g), device_id_type=MESH).start()
    wait_all(retz, C - 1, rtsem.at[1, 1])
    flo, fhi = get_pair(retz)

    def end_z(j, carry):
        out[j] = ff[j] + flo * lz[j] + fhi * hz[j]
        return carry

    lax.fori_loop(0, B, end_z, 0)
    store = pltpu.make_async_copy(out, o_hbm, lsem.at[4])
    store.start()
    for h in halo:
        h.wait_send()
    wait_all(pry, ny - 1, psem.at[0, 0])
    wait_all(prz, nz - 1, psem.at[1, 0])
    wait_all(gry, ny - 1, grsem.at[0, 0])
    wait_all(grz, nz - 1, grsem.at[1, 0])
    wait_all(rety, C - 1, rtsem.at[0, 0])
    wait_all(retz, C - 1, rtsem.at[1, 0])
    store.wait()


def local(nz, ny, tracer, y_speed, z_speed, kappa):
    f32 = jnp.float32
    pad = pltpu.VMEM((B + 2 * HZ, B + 2 * HY, X), f32)
    blk = pltpu.VMEM((B, B, X), f32)
    wgt = pltpu.VMEM((B + 2 * HZ, B + 8, X), f32)

    def tiles(n, rows=8):
        return pltpu.VMEM((n, rows, X), f32)

    scratch = (
        [pad] * 4 + [blk] * 2 + [wgt] * 5
        + [blk] * 5 + [blk] * 5 + [blk] * 6
        + [tiles(C, 24), tiles(C, 24), tiles(ny, 24), tiles(nz, 24)]
        + [tiles(C), tiles(C), tiles(ny), tiles(nz)]
        + [tiles(ny), tiles(ny + 1), tiles(ny + 1), tiles(ny + 1)]
        + [tiles(nz), tiles(nz + 1), tiles(nz + 1), tiles(nz + 1)]
        + [tiles(ny), tiles(ny)]
        + [tiles(C), tiles(C), tiles(C), tiles(C)]
        + [pltpu.SemaphoreType.DMA((5,)), pltpu.SemaphoreType.DMA((24,)),
           pltpu.SemaphoreType.DMA((24,)), pltpu.SemaphoreType.DMA((2, 2)),
           pltpu.SemaphoreType.DMA((2, 2)), pltpu.SemaphoreType.DMA((2, 2))]
    )
    return pl.pallas_call(
        functools.partial(kernel, nz, ny),
        out_shape=jax.ShapeDtypeStruct(tracer.shape, f32),
        in_specs=[pl.BlockSpec(memory_space=pl.ANY)] * 4,
        out_specs=pl.BlockSpec(memory_space=pl.ANY),
        scratch_shapes=scratch,
        compiler_params=pltpu.CompilerParams(
            collective_id=0, has_side_effects=True, vmem_limit_bytes=48 * 1024 * 1024),
    )(tracer, y_speed, z_speed, kappa)


def solution(mesh):
    nz, ny = mesh.shape["gz"], mesh.shape["gy"]
    return jax.shard_map(
        functools.partial(local, nz, ny),
        mesh=mesh,
        in_specs=(P("gz", "gy", None),) * 4,
        out_specs=P("gz", "gy", None),
        check_vma=False,
    )
```

```python
import functools

import jax
import jax.numpy as jnp
from jax import lax
from jax.experimental import pallas as pl
from jax.experimental.pallas import tpu as pltpu
from jax.sharding import PartitionSpec as P

NSUB = 4
RATE = 500.0
HALF_RATE = 250.0
B = 32
X = 128
HZ = 4
HY = 8
C = 8
MESH = pl.DeviceIdType.MESH


def low_rows():
    return lax.broadcasted_iota(jnp.int32, (8, X), 0) < 4


def swap(t):
    return pltpu.roll(t, 4, 0)


def factor(kap, first, last, a_ref, b_ref, inv_ref, lo_ref, hi_ref, tmp_ref):
    e0 = 1.0 + first * kap[0]
    b0 = 1.0 + last * kap[B - 1]
    one = jnp.ones_like(e0)
    inv_ref[0] = e0
    lo_ref[0] = one
    tmp_ref[B - 1] = b0
    hi_ref[B - 1] = one

    def step(s, carry):
        e, eb, ac, bc, kf, kb = carry
        t = B - 1 - s
        kn = kap[s]
        kp = kap[t]
        face = HALF_RATE * (kf + kn)
        a = face / (e + face)
        e = 1.0 + a * e
        ac = ac * a
        faceb = HALF_RATE * (kb + kp)
        b = faceb / (eb + faceb)
        eb = 1.0 + b * eb
        bc = bc * b
        a_ref[s] = a
        inv_ref[s] = e
        lo_ref[s] = ac
        b_ref[t] = b
        tmp_ref[t] = eb
        hi_ref[t] = bc
        return e, eb, ac, bc, kn, kp

    lax.fori_loop(1, B, step, (e0, b0, one, one, kap[0], kap[B - 1]))

    def finish(j, carry):
        inv = 1.0 / (inv_ref[j] + tmp_ref[j] - 1.0)
        inv_ref[j] = inv
        lo_ref[j] = lo_ref[j] * inv
        hi_ref[j] = hi_ref[j] * inv
        return carry

    lax.fori_loop(0, B, finish, 0)


def put_pair(dst, row, first, second):
    low = low_rows()
    for q in range(4):
        f = first[8 * q : 8 * q + 8]
        s = second[8 * q : 8 * q + 8]
        dst[2 * q, row : row + 8] = jnp.where(low, f, swap(s))
        dst[2 * q + 1, row : row + 8] = jnp.where(low, swap(f), s)


def get_pair(src):
    low = low_rows()
    first, second = [], []
    for q in range(4):
        t0 = src[2 * q]
        t1 = src[2 * q + 1]
        first.append(jnp.where(low, t0, swap(t1)))
        second.append(jnp.where(low, swap(t0), t1))
    return jnp.concatenate(first, axis=0), jnp.concatenate(second, axis=0)


def owner_matrix(n, prm, m_ref, y_ref, rf_ref, rb_ref):
    low = low_rows()
    zero = jnp.zeros((8, X), jnp.float32)

    def face(i):
        p = prm[i - 1, 16:24]
        q = prm[i, 16:24]
        k = jnp.where(low, swap(p) + q, p + swap(q))
        return 1.0 / (HALF_RATE * k)

    y_ref[0] = zero
    y_ref[n] = zero
    r0 = prm[0, 0:8]
    rb0 = prm[n - 1, 0:8]
    rf_ref[0] = r0
    rb_ref[n - 1] = rb0
    m_ref[0] = zero
    m_ref[n - 1] = zero

    def step(s, carry):
        r, rb = carry
        z = prm[s, 0:8]
        zt = prm[s, 8:16]
        t = zt / (r + face(s) + swap(z))
        r = z - zt * t
        rf_ref[s] = r
        i = n - 1 - s
        zb = prm[i, 0:8]
        ztb = prm[i, 8:16]
        tb = ztb / (rb + face(i + 1) + swap(zb))
        rb = zb - ztb * tb
        rb_ref[i] = rb
        m_ref[s] = jnp.where(low, m_ref[s], t)
        m_ref[i] = jnp.where(low, tb, m_ref[i])
        return r, rb

    def clear(s, carry):
        m_ref[s] = zero
        return carry

    lax.fori_loop(0, n, clear, 0)
    lax.fori_loop(1, n, step, (r0, rb0))

    def admit(i, carry):
        y_ref[i] = 1.0 / (swap(rf_ref[i - 1]) + face(i) + rb_ref[i])
        return carry

    lax.fori_loop(1, n, admit, 0)


def owner_scan(n, g_ref, m_ref, u_ref, v_ref):
    zero = jnp.zeros((8, X), jnp.float32)
    u_ref[0] = zero
    v_ref[n] = zero

    def step(s, carry):
        u, v = carry
        g = g_ref[s]
        m = m_ref[s]
        u = g - m * swap(g) + m * u
        u_ref[s + 1] = u
        i = n - 1 - s
        gb = g_ref[i]
        mb = m_ref[i]
        v = gb - mb * swap(gb) + mb * v
        v_ref[i] = v
        return u, v

    lax.fori_loop(0, n, step, (zero, zero))


def owner_result(b, u_ref, v_ref, y_ref):
    low = low_rows()
    here = (swap(u_ref[b]) - v_ref[b]) * y_ref[b]
    after = (swap(u_ref[b + 1]) - v_ref[b + 1]) * y_ref[b + 1]
    return jnp.where(low, here, -swap(after))


def local_scan(r_ref, a_ref, b_ref, f_ref, g_ref, inv_ref):
    r0 = r_ref[0]
    rb0 = r_ref[B - 1]
    f_ref[0] = r0
    g_ref[B - 1] = jnp.zeros_like(r0)

    def step(s, carry):
        f, g = carry
        t = B - 1 - s
        f = r_ref[s] + a_ref[s] * f
        bg = b_ref[t] * g
        g = r_ref[t] + bg
        f_ref[s] = f
        g_ref[t] = bg
        return f, g

    f, g = lax.fori_loop(1, B, step, (r0, rb0))
    return g * inv_ref[0], f * inv_ref[B - 1]


def kernel(nz, ny, *refs):
    (c_hbm, v_hbm, w_hbm, k_hbm, o_hbm,
     ca, cb, vv, ww, kz, ky, k0, cym, cyp, czm, czp,
     ay, by, iy, ly, hy, az, bz, iz, lz, hz, tmp, rr, ff, gg, uz, out,
     psy, psz, pry, prz, gsy, gsz, gry, grz,
     my, yy, uy, vy, mz, yz, uo, vo, rf, rb,
     rsy, rsz, rety, retz,
     lsem, hsend, hrecv, psem, grsem, rtsem) = refs
    p = lax.axis_index("gz")
    g = lax.axis_index("gy")

    def zi(k):
        return lax.rem(p + k + nz, nz)

    def yi(k):
        return lax.rem(g + k + ny, ny)

    bar = pltpu.get_barrier_semaphore()

    def greet(pz, gy):
        pl.semaphore_signal(bar, inc=1, device_id=(pz, gy), device_id_type=MESH)

    for dz in (1, -1):
        for dy in (1, -1):
            greet(zi(dz), yi(dy))
    for k in range(1, nz):
        greet(zi(k), g)
    for k in range(1, ny):
        greet(p, yi(k))

    loads = [
        pltpu.make_async_copy(k_hbm, kz, lsem.at[0]),
        pltpu.make_async_copy(c_hbm, ca.at[HZ : HZ + B, HY : HY + B], lsem.at[1]),
        pltpu.make_async_copy(v_hbm, vv.at[HZ : HZ + B, HY : HY + B], lsem.at[2]),
        pltpu.make_async_copy(w_hbm, ww.at[HZ : HZ + B, HY : HY + B], lsem.at[3]),
    ]
    for ld in loads:
        ld.start()

    pl.semaphore_wait(bar, 4 + (nz - 1) + (ny - 1))

    def near(d, size, pad, width):
        if d == 0:
            return slice(0, size), slice(pad, pad + size)
        if d > 0:
            return slice(size - width, size), slice(pad - width, pad)
        return slice(0, width), slice(pad + size, pad + size + width)

    halo = []
    for dz, dy in ((0, 1), (0, -1), (1, 0), (-1, 0), (1, 1), (1, -1), (-1, 1), (-1, -1)):
        for src, dst, wz, wy in ((c_hbm, ca, 4, 4), (v_hbm, vv, 3, 4), (w_hbm, ww, 4, 3)):
            if dz and dy:
                wz, wy = 3, 3
            zs, zd = near(dz, B, HZ, wz)
            ys, yd = near(dy, B, HY, wy)
            i = len(halo)
            halo.append(pltpu.make_async_remote_copy(
                src.at[zs, ys], dst.at[zd, yd], hsend.at[i], hrecv.at[i],
                device_id=(zi(dz), yi(dy)), device_id_type=MESH))
    for h in halo:
        h.start()

    loads[0].wait()
    kflat = kz.reshape(B * B, X)

    def turn(j, carry):
        ky[j] = kflat[pl.ds(j, B, stride=B), :]
        return carry

    lax.fori_loop(0, B, turn, 0)
    yfirst = jnp.where(g == 0, RATE, 0.0).astype(jnp.float32)
    ylast = jnp.where(g == ny - 1, RATE, 0.0).astype(jnp.float32)
    zfirst = jnp.where(p == 0, RATE, 0.0).astype(jnp.float32)
    zlast = jnp.where(p == nz - 1, RATE, 0.0).astype(jnp.float32)

    factor(ky, yfirst, ylast, ay, by, iy, ly, hy, tmp)
    put_pair(psy, 0, ly[0], hy[B - 1])
    put_pair(psy, 8, hy[0], hy[0])
    put_pair(psy, 16, ky[0], ky[B - 1])
    pry[g] = psy[lax.rem(g, C)]

    def to_y(src, dst, sem, k):
        return pltpu.make_async_remote_copy(
            src.at[lax.rem(g + k, C)], dst.at[g], sem.at[0], sem.at[1],
            device_id=(p, yi(k)), device_id_type=MESH)

    def to_z(src, dst, sem, k):
        return pltpu.make_async_remote_copy(
            src.at[lax.rem(p + k, C)], dst.at[p], sem.at[0], sem.at[1],
            device_id=(zi(k), g), device_id_type=MESH)

    def wait_all(ref, count, sem):
        part = ref.at[pl.ds(0, count)]
        pltpu.make_async_copy(part, part, sem).wait()

    for k in range(1, ny):
        to_y(psy, pry, psem.at[0], k).start()

    factor(kz, zfirst, zlast, az, bz, iz, lz, hz, tmp)
    put_pair(psz, 0, lz[0], hz[B - 1])
    put_pair(psz, 8, hz[0], hz[0])
    put_pair(psz, 16, kz[0], kz[B - 1])
    prz[p] = psz[lax.rem(p, C)]

    for ld in loads[1:]:
        ld.wait()
    for h in halo:
        h.wait_recv()
    for k in range(1, nz):
        to_z(psz, prz, psem.at[1], k).start()

    zero3 = jnp.zeros((HZ, B + 2 * HY, X), jnp.float32)
    zero_row = jnp.zeros((HY, X), jnp.float32)

    def zero_y(at):
        def body(z, carry):
            for ref in (ca, vv, ww):
                ref[z, at : at + HY] = zero_row
            return carry

        lax.fori_loop(0, B + 2 * HZ, body, 0)

    @pl.when(p == 0)
    def _():
        for ref in (ca, vv, ww):
            ref[0:HZ] = zero3

    @pl.when(p == nz - 1)
    def _():
        for ref in (ca, vv, ww):
            ref[HZ + B : 2 * HZ + B] = zero3

    @pl.when(g == 0)
    def _():
        zero_y(0)

    @pl.when(g == ny - 1)
    def _():
        zero_y(HY + B)

    LO, N5 = 4, B + 8

    def z_face(a, b):
        f = 0.5 * (a + b)
        return jnp.maximum(f, 0.0), jnp.minimum(f, 0.0)

    def weights(z, carry):
        wc, zm_pos, zm_neg = carry
        wp = ww[z + 1, LO : LO + N5]
        zp_pos, zp_neg = z_face(wc, wp)
        vc = vv[z, LO : LO + N5]
        ym_pos, ym_neg = z_face(vv[z, LO - 1 : LO - 1 + N5], vc)
        yp_pos, yp_neg = z_face(vc, vv[z, LO + 1 : LO + 1 + N5])
        cyp[z] = yp_neg
        cym[z] = ym_pos
        czp[z] = zp_neg
        czm[z] = zm_pos
        k0[z] = ((1.0 - yp_pos) + (ym_neg - zp_pos)) + zm_neg
        return wp, zp_pos, zp_neg

    w1 = ww[1, LO : LO + N5]
    lax.fori_loop(1, B + 2 * HZ - 1, weights, (w1, *z_face(ww[0, LO : LO + N5], w1)), unroll=2)

    wrefs = (k0, cym, cyp, czm, czp)
    zero_w = jnp.zeros((HZ - 1, N5, X), jnp.float32)

    def zero_wy(at):
        def body(z, carry):
            for ref in wrefs:
                ref[z, at : at + 4] = jnp.zeros((4, X), jnp.float32)
            return carry

        lax.fori_loop(1, B + 2 * HZ - 1, body, 0)

    @pl.when(p == 0)
    def _():
        for ref in wrefs:
            ref[1:HZ] = zero_w

    @pl.when(p == nz - 1)
    def _():
        for ref in wrefs:
            ref[HZ + B : 2 * HZ + B - 1] = zero_w

    @pl.when(g == 0)
    def _():
        zero_wy(0)

    @pl.when(g == ny - 1)
    def _():
        zero_wy(4 + B)

    for s in range(1, NSUB + 1):
        src, dst = (ca, cb) if s % 2 == 1 else (cb, ca)

        def sub(z, carry, src=src, dst=dst):
            new = ((k0[z] * src[z, LO : LO + N5]
                    + cym[z] * src[z, LO - 1 : LO - 1 + N5])
                   - (cyp[z] * src[z, LO + 1 : LO + 1 + N5]
                      - czm[z] * src[z - 1, LO : LO + N5])
                   - czp[z] * src[z + 1, LO : LO + N5])
            dst[z, LO : LO + N5] = new
            return carry

        lax.fori_loop(s, B + 2 * HZ - s, sub, 0)

    cflat = ca.reshape((B + 2 * HZ) * (B + 2 * HY), X)

    def turn_r(j, carry):
        rr[j] = cflat[pl.ds(HZ * (B + 2 * HY) + HY + j, B, stride=B + 2 * HY), :]
        return carry

    lax.fori_loop(0, B, turn_r, 0)
    g0, gl = local_scan(rr, ay, by, ff, gg, iy)
    put_pair(gsy, 0, g0, gl)
    gry[g] = gsy[lax.rem(g, C)]
    for k in range(1, ny):
        to_y(gsy, gry, grsem.at[0], k).start()

    wait_all(pry, ny - 1, psem.at[0, 1])
    owner_matrix(ny, pry, my, yy, rf, rb)

    def base(j, carry):
        ff[j] = (ff[j] + gg[j]) * inv_now[j]
        return carry

    inv_now = iy
    lax.fori_loop(0, B, base, 0)

    wait_all(gry, ny - 1, grsem.at[0, 1])
    owner_scan(ny, gry, my, uy, vy)
    yc = lax.rem(g, C)
    yb = g - yc
    rety[yc] = owner_result(g, uy, vy, yy)
    for m in range(1, C):
        b = yb + lax.rem(yc + m, C)
        rsy[m] = owner_result(b, uy, vy, yy)
        pltpu.make_async_remote_copy(
            rsy.at[m], rety.at[yc], rtsem.at[0, 0], rtsem.at[0, 1],
            device_id=(p, b), device_id_type=MESH).start()

    wait_all(prz, nz - 1, psem.at[1, 1])
    owner_matrix(nz, prz, mz, yz, rf, rb)

    wait_all(rety, C - 1, rtsem.at[0, 1])
    flo, fhi = get_pair(rety)
    uflat = uz.reshape(B * B, X)

    def end_y(j, carry):
        uflat[pl.ds(j, B, stride=B), :] = ff[j] + flo * ly[j] + fhi * hy[j]
        return carry

    lax.fori_loop(0, B, end_y, 0)

    g0, gl = local_scan(uz, az, bz, ff, gg, iz)
    put_pair(gsz, 0, g0, gl)
    grz[p] = gsz[lax.rem(p, C)]
    for k in range(1, nz):
        to_z(gsz, grz, grsem.at[1], k).start()
    inv_now = iz

    def base_z(j, carry):
        ff[j] = (ff[j] + gg[j]) * iz[j]
        return carry

    lax.fori_loop(0, B, base_z, 0)
    wait_all(grz, nz - 1, grsem.at[1, 1])
    owner_scan(nz, grz, mz, uo, vo)
    zc = lax.rem(p, C)
    retz[zc] = owner_result(p, uo, vo, yz)
    others = [o for o in range(-(C // 2), C // 2) if o != 0]
    for m, o in enumerate(others):
        b = zi(o)
        rsz[m] = owner_result(b, uo, vo, yz)
        pltpu.make_async_remote_copy(
            rsz.at[m], retz.at[zc], rtsem.at[1, 0], rtsem.at[1, 1],
            device_id=(b, g), device_id_type=MESH).start()
    wait_all(retz, C - 1, rtsem.at[1, 1])
    flo, fhi = get_pair(retz)

    def end_z(j, carry):
        out[j] = ff[j] + flo * lz[j] + fhi * hz[j]
        return carry

    lax.fori_loop(0, B, end_z, 0)
    store = pltpu.make_async_copy(out, o_hbm, lsem.at[4])
    store.start()
    for h in halo:
        h.wait_send()
    wait_all(pry, ny - 1, psem.at[0, 0])
    wait_all(prz, nz - 1, psem.at[1, 0])
    wait_all(gry, ny - 1, grsem.at[0, 0])
    wait_all(grz, nz - 1, grsem.at[1, 0])
    wait_all(rety, C - 1, rtsem.at[0, 0])
    wait_all(retz, C - 1, rtsem.at[1, 0])
    store.wait()


def local(nz, ny, tracer, y_speed, z_speed, kappa):
    f32 = jnp.float32
    pad = pltpu.VMEM((B + 2 * HZ, B + 2 * HY, X), f32)
    blk = pltpu.VMEM((B, B, X), f32)
    wgt = pltpu.VMEM((B + 2 * HZ, B + 8, X), f32)

    def tiles(n, rows=8):
        return pltpu.VMEM((n, rows, X), f32)

    scratch = (
        [pad] * 4 + [blk] * 2 + [wgt] * 5
        + [blk] * 5 + [blk] * 5 + [blk] * 6
        + [tiles(C, 24), tiles(C, 24), tiles(ny, 24), tiles(nz, 24)]
        + [tiles(C), tiles(C), tiles(ny), tiles(nz)]
        + [tiles(ny), tiles(ny + 1), tiles(ny + 1), tiles(ny + 1)]
        + [tiles(nz), tiles(nz + 1), tiles(nz + 1), tiles(nz + 1)]
        + [tiles(ny), tiles(ny)]
        + [tiles(C), tiles(C), tiles(C), tiles(C)]
        + [pltpu.SemaphoreType.DMA((5,)), pltpu.SemaphoreType.DMA((24,)),
           pltpu.SemaphoreType.DMA((24,)), pltpu.SemaphoreType.DMA((2, 2)),
           pltpu.SemaphoreType.DMA((2, 2)), pltpu.SemaphoreType.DMA((2, 2))]
    )
    return pl.pallas_call(
        functools.partial(kernel, nz, ny),
        out_shape=jax.ShapeDtypeStruct(tracer.shape, f32),
        in_specs=[pl.BlockSpec(memory_space=pl.ANY)] * 4,
        out_specs=pl.BlockSpec(memory_space=pl.ANY),
        scratch_shapes=scratch,
        compiler_params=pltpu.CompilerParams(
            collective_id=0, has_side_effects=True, vmem_limit_bytes=67043328),
    )(tracer, y_speed, z_speed, kappa)


def solution(mesh):
    nz, ny = mesh.shape["gz"], mesh.shape["gy"]
    return jax.shard_map(
        functools.partial(local, nz, ny),
        mesh=mesh,
        in_specs=(P("gz", "gy", None),) * 4,
        out_specs=P("gz", "gy", None),
        check_vma=False,
    )
```

```python
import functools

import jax
import jax.numpy as jnp
from jax import lax
from jax.experimental import pallas as pl
from jax.experimental.pallas import tpu as pltpu
from jax.sharding import PartitionSpec as P

NSUB = 4
RATE = 500.0
HALF_RATE = 250.0
B = 32
X = 128
HZ = 4
HY = 8
C = 8
PR = 12
OUT = 8
MESH = pl.DeviceIdType.MESH


def low_rows():
    return lax.broadcasted_iota(jnp.int32, (8, X), 0) < 4


def swap(t):
    return pltpu.roll(t, 4, 0)


def factor(kap, first, last, a_ref, b_ref, inv_ref, lo_ref, hi_ref, tmp_ref):
    e0 = 1.0 + first * kap[0]
    b0 = 1.0 + last * kap[B - 1]
    one = jnp.ones_like(e0)
    inv_ref[0] = e0
    lo_ref[0] = one
    tmp_ref[B - 1] = b0
    hi_ref[B - 1] = one

    def step(s, carry):
        e, eb, ac, bc, kf, kb = carry
        t = B - 1 - s
        kn = kap[s]
        kp = kap[t]
        face = HALF_RATE * (kf + kn)
        a = face / (e + face)
        e = 1.0 + a * e
        ac = ac * a
        faceb = HALF_RATE * (kb + kp)
        b = faceb / (eb + faceb)
        eb = 1.0 + b * eb
        bc = bc * b
        a_ref[s] = a
        inv_ref[s] = e
        lo_ref[s] = ac
        b_ref[t] = b
        tmp_ref[t] = eb
        hi_ref[t] = bc
        return e, eb, ac, bc, kn, kp

    lax.fori_loop(1, B, step, (e0, b0, one, one, kap[0], kap[B - 1]))

    def finish(j, carry):
        inv = 1.0 / (inv_ref[j] + tmp_ref[j] - 1.0)
        inv_ref[j] = inv
        lo_ref[j] = lo_ref[j] * inv
        hi_ref[j] = hi_ref[j] * inv
        return carry

    lax.fori_loop(0, B, finish, 0)


def put_pair(dst, row, first, second):
    low = low_rows()
    for q in range(4):
        f = first[8 * q : 8 * q + 8]
        s = second[8 * q : 8 * q + 8]
        dst[2 * q, row : row + 8] = jnp.where(low, f, swap(s))
        dst[2 * q + 1, row : row + 8] = jnp.where(low, swap(f), s)


def get_pair(src):
    low = low_rows()
    first, second = [], []
    for q in range(4):
        t0 = src[2 * q]
        t1 = src[2 * q + 1]
        first.append(jnp.where(low, t0, swap(t1)))
        second.append(jnp.where(low, swap(t0), t1))
    return jnp.concatenate(first, axis=0), jnp.concatenate(second, axis=0)


def owner_matrix(n, prm, m_ref, y_ref, rf_ref, rb_ref):
    low = low_rows()
    zero = jnp.zeros((8, X), jnp.float32)

    def block(i):
        c = prm[i, 8:16]
        return prm[i, 0:8], jnp.where(low, c, swap(c))

    y_ref[0] = zero
    y_ref[n] = zero
    r0 = prm[0, 0:8]
    rb0 = prm[n - 1, 0:8]
    rf_ref[0] = r0
    rb_ref[n - 1] = rb0
    m_ref[0] = zero
    m_ref[n - 1] = zero

    def step(s, carry):
        r, rb = carry
        z, zt = block(s)
        t = zt / (r + swap(z))
        r = z - zt * t
        rf_ref[s] = r
        i = n - 1 - s
        zb, ztb = block(i)
        tb = ztb / (rb + swap(zb))
        rb = zb - ztb * tb
        rb_ref[i] = rb
        m_ref[s] = jnp.where(low, m_ref[s], t)
        m_ref[i] = jnp.where(low, tb, m_ref[i])
        return r, rb

    def clear(s, carry):
        m_ref[s] = zero
        return carry

    lax.fori_loop(0, n, clear, 0)
    lax.fori_loop(1, n, step, (r0, rb0))

    def admit(i, carry):
        y_ref[i] = 1.0 / (swap(rf_ref[i - 1]) + rb_ref[i])
        return carry

    lax.fori_loop(1, n, admit, 0)


def owner_scan(n, g_ref, m_ref, u_ref, v_ref):
    zero = jnp.zeros((8, X), jnp.float32)
    u_ref[0] = zero
    v_ref[n] = zero

    def step(s, carry):
        u, v = carry
        g = g_ref[s]
        m = m_ref[s]
        u = g - m * swap(g) + m * u
        u_ref[s + 1] = u
        i = n - 1 - s
        gb = g_ref[i]
        mb = m_ref[i]
        v = gb - mb * swap(gb) + mb * v
        v_ref[i] = v
        return u, v

    lax.fori_loop(0, n, step, (zero, zero))


def owner_result(b, u_ref, v_ref, y_ref):
    low = low_rows()
    here = (swap(u_ref[b]) - v_ref[b]) * y_ref[b]
    after = (swap(u_ref[b + 1]) - v_ref[b + 1]) * y_ref[b + 1]
    return jnp.where(low, here, -swap(after))


def local_scan(r_ref, a_ref, b_ref, f_ref, g_ref, inv_ref):
    r0 = r_ref[0]
    rb0 = r_ref[B - 1]
    f_ref[0] = r0
    g_ref[B - 1] = jnp.zeros_like(r0)

    def step(s, carry):
        f, g = carry
        t = B - 1 - s
        f = r_ref[s] + a_ref[s] * f
        bg = b_ref[t] * g
        g = r_ref[t] + bg
        f_ref[s] = f
        g_ref[t] = bg
        return f, g

    f, g = lax.fori_loop(1, B, step, (r0, rb0))
    return g * inv_ref[0], f * inv_ref[B - 1]


def kernel(nz, ny, *refs):
    (c_hbm, v_hbm, w_hbm, k_hbm, o_hbm,
     ca, cb, vv, ww, kz, ky, k0, cym, cyp, czm, czp,
     ay, by, iy, ly, hy, az, bz, iz, lz, hz, tmp, rr, ff, gg, uz, out,
     psy, psz, pry, prz, gsy, gsz, gry, grz,
     my, yy, uy, vy, mz, yz, uo, vo, rf, rb,
     rsy, rsz, rety, retz,
     kye, kze, lsem, hsend, hrecv, psem, grsem, rtsem, ksem) = refs
    p = lax.axis_index("gz")
    g = lax.axis_index("gy")

    def zi(k):
        return lax.rem(p + k + nz, nz)

    def yi(k):
        return lax.rem(g + k + ny, ny)

    bar = pltpu.get_barrier_semaphore()

    def greet(pz, gy):
        pl.semaphore_signal(bar, inc=1, device_id=(pz, gy), device_id_type=MESH)

    for dz in (1, -1):
        for dy in (1, -1):
            greet(zi(dz), yi(dy))
    for k in range(1, nz):
        greet(zi(k), g)
    for k in range(1, ny):
        greet(p, yi(k))

    loads = [
        pltpu.make_async_copy(k_hbm, kz, lsem.at[0]),
        pltpu.make_async_copy(c_hbm, ca.at[HZ : HZ + B, HY : HY + B], lsem.at[1]),
        pltpu.make_async_copy(v_hbm, vv.at[HZ : HZ + B, HY : HY + B], lsem.at[2]),
        pltpu.make_async_copy(w_hbm, ww.at[HZ : HZ + B, HY : HY + B], lsem.at[3]),
    ]
    for ld in loads:
        ld.start()

    pl.semaphore_wait(bar, 4 + (nz - 1) + (ny - 1))

    def near(d, size, pad, width):
        if d == 0:
            return slice(0, size), slice(pad, pad + size)
        if d > 0:
            return slice(size - width, size), slice(pad - width, pad)
        return slice(0, width), slice(pad + size, pad + size + width)

    halo = []
    for dz, dy in ((0, 1), (0, -1), (1, 0), (-1, 0), (1, 1), (1, -1), (-1, 1), (-1, -1)):
        for src, dst, wz, wy in ((c_hbm, ca, 4, 4), (v_hbm, vv, 3, 4), (w_hbm, ww, 4, 3)):
            if dz and dy:
                wz, wy = 3, 3
            zs, zd = near(dz, B, HZ, wz)
            ys, yd = near(dy, B, HY, wy)
            i = len(halo)
            halo.append(pltpu.make_async_remote_copy(
                src.at[zs, ys], dst.at[zd, yd], hsend.at[i], hrecv.at[i],
                device_id=(zi(dz), yi(dy)), device_id_type=MESH))
    edges = [
        pltpu.make_async_remote_copy(
            k_hbm.at[:, B - 1 : B], kye.at[:, 0:1], ksem.at[0], ksem.at[1],
            device_id=(p, yi(1)), device_id_type=MESH),
        pltpu.make_async_remote_copy(
            k_hbm.at[B - 1], kze, ksem.at[2], ksem.at[3],
            device_id=(zi(1), g), device_id_type=MESH),
    ]
    for h in edges + halo:
        h.start()

    loads[0].wait()
    kflat = kz.reshape(B * B, X)

    def turn(j, carry):
        ky[j] = kflat[pl.ds(j, B, stride=B), :]
        return carry

    lax.fori_loop(0, B, turn, 0)
    yfirst = jnp.where(g == 0, RATE, 0.0).astype(jnp.float32)
    ylast = jnp.where(g == ny - 1, RATE, 0.0).astype(jnp.float32)
    zfirst = jnp.where(p == 0, RATE, 0.0).astype(jnp.float32)
    zlast = jnp.where(p == nz - 1, RATE, 0.0).astype(jnp.float32)

    factor(ky, yfirst, ylast, ay, by, iy, ly, hy, tmp)
    edges[0].wait_recv()
    below = kye.reshape(B * 8, X)[pl.ds(0, B, stride=8), :]
    put_pair(psy, 0, ly[0] + 1.0 / (HALF_RATE * (below + ky[0])), hy[B - 1])
    put_pair(psy, 8, hy[0], hy[0])
    pry[g] = psy[lax.rem(g, C)]

    def to_y(src, dst, sem, k):
        return pltpu.make_async_remote_copy(
            src.at[lax.rem(g + k, C)], dst.at[g], sem.at[0], sem.at[1],
            device_id=(p, yi(k)), device_id_type=MESH)

    def to_z(src, dst, sem, k):
        return pltpu.make_async_remote_copy(
            src.at[lax.rem(p + k, C)], dst.at[p], sem.at[0], sem.at[1],
            device_id=(zi(k), g), device_id_type=MESH)

    def wait_all(ref, count, sem):
        part = ref.at[pl.ds(0, count)]
        pltpu.make_async_copy(part, part, sem).wait()

    for k in range(1, ny):
        to_y(psy.at[:, 0:PR], pry.at[:, 0:PR], psem.at[0], k).start()

    factor(kz, zfirst, zlast, az, bz, iz, lz, hz, tmp)
    edges[1].wait_recv()
    put_pair(psz, 0, lz[0] + 1.0 / (HALF_RATE * (kze[...] + kz[0])), hz[B - 1])
    put_pair(psz, 8, hz[0], hz[0])
    prz[p] = psz[lax.rem(p, C)]

    for ld in loads[1:]:
        ld.wait()
    for h in halo:
        h.wait_recv()
    for k in range(1, nz):
        to_z(psz.at[:, 0:PR], prz.at[:, 0:PR], psem.at[1], k).start()

    zero3 = jnp.zeros((HZ, B + 2 * HY, X), jnp.float32)
    zero_row = jnp.zeros((HY, X), jnp.float32)

    def zero_y(at):
        def body(z, carry):
            for ref in (ca, vv, ww):
                ref[z, at : at + HY] = zero_row
            return carry

        lax.fori_loop(0, B + 2 * HZ, body, 0)

    @pl.when(p == 0)
    def _():
        for ref in (ca, vv, ww):
            ref[0:HZ] = zero3

    @pl.when(p == nz - 1)
    def _():
        for ref in (ca, vv, ww):
            ref[HZ + B : 2 * HZ + B] = zero3

    @pl.when(g == 0)
    def _():
        zero_y(0)

    @pl.when(g == ny - 1)
    def _():
        zero_y(HY + B)

    LO, N5 = 4, B + 8

    def z_face(a, b):
        f = 0.5 * (a + b)
        return jnp.maximum(f, 0.0), jnp.minimum(f, 0.0)

    def weights(z, carry):
        wc, zm_pos, zm_neg = carry
        wp = ww[z + 1, LO : LO + N5]
        zp_pos, zp_neg = z_face(wc, wp)
        vc = vv[z, LO : LO + N5]
        ym_pos, ym_neg = z_face(vv[z, LO - 1 : LO - 1 + N5], vc)
        yp_pos, yp_neg = z_face(vc, vv[z, LO + 1 : LO + 1 + N5])
        cyp[z] = yp_neg
        cym[z] = ym_pos
        czp[z] = zp_neg
        czm[z] = zm_pos
        k0[z] = ((1.0 - yp_pos) + (ym_neg - zp_pos)) + zm_neg
        return wp, zp_pos, zp_neg

    w1 = ww[1, LO : LO + N5]
    lax.fori_loop(1, B + 2 * HZ - 1, weights, (w1, *z_face(ww[0, LO : LO + N5], w1)), unroll=2)

    wrefs = (k0, cym, cyp, czm, czp)
    zero_w = jnp.zeros((HZ - 1, N5, X), jnp.float32)

    def zero_wy(at):
        def body(z, carry):
            for ref in wrefs:
                ref[z, at : at + 4] = jnp.zeros((4, X), jnp.float32)
            return carry

        lax.fori_loop(1, B + 2 * HZ - 1, body, 0)

    @pl.when(p == 0)
    def _():
        for ref in wrefs:
            ref[1:HZ] = zero_w

    @pl.when(p == nz - 1)
    def _():
        for ref in wrefs:
            ref[HZ + B : 2 * HZ + B - 1] = zero_w

    @pl.when(g == 0)
    def _():
        zero_wy(0)

    @pl.when(g == ny - 1)
    def _():
        zero_wy(4 + B)

    for s in range(1, NSUB):
        src, dst = (ca, cb) if s % 2 == 1 else (cb, ca)

        def sub(z, carry, src=src, dst=dst):
            new = ((k0[z] * src[z, LO : LO + N5]
                    + cym[z] * src[z, LO - 1 : LO - 1 + N5])
                   - (cyp[z] * src[z, LO + 1 : LO + 1 + N5]
                      - czm[z] * src[z - 1, LO : LO + N5])
                   - czp[z] * src[z + 1, LO : LO + N5])
            dst[z, LO : LO + N5] = new
            return carry

        lax.fori_loop(s, B + 2 * HZ - s, sub, 0)

    src = cb if NSUB % 2 == 0 else ca
    rflat = rr.reshape(B * B, X)

    def last(z, carry):
        at, up = slice(HY, HY + B), slice(4, 4 + B)
        new = ((k0[z, up] * src[z, at]
                + cym[z, up] * src[z, HY - 1 : HY - 1 + B])
               - (cyp[z, up] * src[z, HY + 1 : HY + 1 + B]
                  - czm[z, up] * src[z - 1, at])
               - czp[z, up] * src[z + 1, at])
        rflat[pl.ds(z - HZ, B, stride=B), :] = new
        return carry

    lax.fori_loop(HZ, HZ + B, last, 0)

    g0, gl = local_scan(rr, ay, by, ff, gg, iy)
    put_pair(gsy, 0, g0, gl)
    gry[g] = gsy[lax.rem(g, C)]
    for k in range(1, ny):
        to_y(gsy, gry, grsem.at[0], k).start()

    wait_all(pry.at[:, 0:PR], ny - 1, psem.at[0, 1])
    owner_matrix(ny, pry, my, yy, rf, rb)

    def base(j, carry):
        ff[j] = (ff[j] + gg[j]) * inv_now[j]
        return carry

    inv_now = iy
    lax.fori_loop(0, B, base, 0)

    wait_all(gry, ny - 1, grsem.at[0, 1])
    owner_scan(ny, gry, my, uy, vy)
    yc = lax.rem(g, C)
    yb = g - yc
    rety[yc] = owner_result(g, uy, vy, yy)
    for m in range(1, C):
        b = yb + lax.rem(yc + m, C)
        rsy[m] = owner_result(b, uy, vy, yy)
        pltpu.make_async_remote_copy(
            rsy.at[m], rety.at[yc], rtsem.at[0, 0], rtsem.at[0, 1],
            device_id=(p, b), device_id_type=MESH).start()

    wait_all(prz.at[:, 0:PR], nz - 1, psem.at[1, 1])
    owner_matrix(nz, prz, mz, yz, rf, rb)

    wait_all(rety, C - 1, rtsem.at[0, 1])
    flo, fhi = get_pair(rety)
    uflat = uz.reshape(B * B, X)

    def end_y(j, carry):
        uflat[pl.ds(j, B, stride=B), :] = ff[j] + flo * ly[j] + fhi * hy[j]
        return carry

    lax.fori_loop(0, B, end_y, 0)

    g0, gl = local_scan(uz, az, bz, ff, gg, iz)
    put_pair(gsz, 0, g0, gl)
    grz[p] = gsz[lax.rem(p, C)]
    for k in range(1, nz):
        to_z(gsz, grz, grsem.at[1], k).start()
    inv_now = iz

    def base_z(j, carry):
        ff[j] = (ff[j] + gg[j]) * iz[j]
        return carry

    lax.fori_loop(0, B, base_z, 0)
    wait_all(grz, nz - 1, grsem.at[1, 1])
    owner_scan(nz, grz, mz, uo, vo)
    zc = lax.rem(p, C)
    retz[zc] = owner_result(p, uo, vo, yz)
    others = [o for o in range(-(C // 2), C // 2) if o != 0]
    for m, o in enumerate(others):
        b = zi(o)
        rsz[m] = owner_result(b, uo, vo, yz)
        pltpu.make_async_remote_copy(
            rsz.at[m], retz.at[zc], rtsem.at[1, 0], rtsem.at[1, 1],
            device_id=(b, g), device_id_type=MESH).start()
    wait_all(retz, C - 1, rtsem.at[1, 1])
    flo, fhi = get_pair(retz)

    def end_z(j, carry):
        out[j] = ff[j] + flo * lz[j] + fhi * hz[j]
        return carry

    stores = []
    for j in range(0, B, OUT):
        lax.fori_loop(j, j + OUT, end_z, 0)
        st = pltpu.make_async_copy(
            out.at[j : j + OUT], o_hbm.at[j : j + OUT], lsem.at[4 + j // OUT])
        st.start()
        stores.append(st)
    for h in edges + halo:
        h.wait_send()
    wait_all(pry.at[:, 0:PR], ny - 1, psem.at[0, 0])
    wait_all(prz.at[:, 0:PR], nz - 1, psem.at[1, 0])
    wait_all(gry, ny - 1, grsem.at[0, 0])
    wait_all(grz, nz - 1, grsem.at[1, 0])
    wait_all(rety, C - 1, rtsem.at[0, 0])
    wait_all(retz, C - 1, rtsem.at[1, 0])
    for st in stores:
        st.wait()


def local(nz, ny, tracer, y_speed, z_speed, kappa):
    f32 = jnp.float32
    pad = pltpu.VMEM((B + 2 * HZ, B + 2 * HY, X), f32)
    blk = pltpu.VMEM((B, B, X), f32)
    wgt = pltpu.VMEM((B + 2 * HZ, B + 8, X), f32)

    def tiles(n, rows=8):
        return pltpu.VMEM((n, rows, X), f32)

    scratch = (
        [pad] * 4 + [blk] * 2 + [wgt] * 5
        + [blk] * 5 + [blk] * 5 + [blk] * 6
        + [tiles(C, 16), tiles(C, 16), tiles(ny, 16), tiles(nz, 16)]
        + [tiles(C), tiles(C), tiles(ny), tiles(nz)]
        + [tiles(ny), tiles(ny + 1), tiles(ny + 1), tiles(ny + 1)]
        + [tiles(nz), tiles(nz + 1), tiles(nz + 1), tiles(nz + 1)]
        + [tiles(ny), tiles(ny)]
        + [tiles(C), tiles(C), tiles(C), tiles(C)]
        + [tiles(B), pltpu.VMEM((B, X), f32), pltpu.SemaphoreType.DMA((4 + B // OUT,)), pltpu.SemaphoreType.DMA((24,)),
           pltpu.SemaphoreType.DMA((24,)), pltpu.SemaphoreType.DMA((2, 2)),
           pltpu.SemaphoreType.DMA((2, 2)), pltpu.SemaphoreType.DMA((2, 2)),
           pltpu.SemaphoreType.DMA((4,))]
    )
    return pl.pallas_call(
        functools.partial(kernel, nz, ny),
        out_shape=jax.ShapeDtypeStruct(tracer.shape, f32),
        in_specs=[pl.BlockSpec(memory_space=pl.ANY)] * 4,
        out_specs=pl.BlockSpec(memory_space=pl.ANY),
        scratch_shapes=scratch,
        compiler_params=pltpu.CompilerParams(
            collective_id=0, has_side_effects=True, vmem_limit_bytes=56000000),
    )(tracer, y_speed, z_speed, kappa)


def solution(mesh):
    nz, ny = mesh.shape["gz"], mesh.shape["gy"]
    return jax.shard_map(
        functools.partial(local, nz, ny),
        mesh=mesh,
        in_specs=(P("gz", "gy", None),) * 4,
        out_specs=P("gz", "gy", None),
        check_vma=False,
    )
```

```python
import functools

import jax
import jax.numpy as jnp
from jax import lax
from jax.experimental import pallas as pl
from jax.experimental.pallas import tpu as pltpu
from jax.sharding import PartitionSpec as P

NSUB = 4
RATE = 500.0
HALF_RATE = 250.0
B = 32
X = 128
HZ = 4
HY = 8
C = 8
PR = 12
OUT = 8
MESH = pl.DeviceIdType.MESH


def low_rows():
    return lax.broadcasted_iota(jnp.int32, (8, X), 0) < 4


def swap(t):
    return pltpu.roll(t, 4, 0)


def factor(kap, first, last, a_ref, b_ref, inv_ref, lo_ref, hi_ref, tmp_ref):
    e0 = 1.0 + first * kap[0]
    b0 = 1.0 + last * kap[B - 1]
    one = jnp.ones_like(e0)
    inv_ref[0] = e0
    lo_ref[0] = one
    tmp_ref[B - 1] = b0
    hi_ref[B - 1] = one

    def step(s, carry):
        e, eb, ac, bc, kf, kb = carry
        t = B - 1 - s
        kn = kap[s]
        kp = kap[t]
        face = HALF_RATE * (kf + kn)
        a = face / (e + face)
        e = 1.0 + a * e
        ac = ac * a
        faceb = HALF_RATE * (kb + kp)
        b = faceb / (eb + faceb)
        eb = 1.0 + b * eb
        bc = bc * b
        a_ref[s] = a
        inv_ref[s] = e
        lo_ref[s] = ac
        b_ref[t] = b
        tmp_ref[t] = eb
        hi_ref[t] = bc
        return e, eb, ac, bc, kn, kp

    lax.fori_loop(1, B, step, (e0, b0, one, one, kap[0], kap[B - 1]))

    def finish(j, carry):
        inv = 1.0 / (inv_ref[j] + tmp_ref[j] - 1.0)
        inv_ref[j] = inv
        lo_ref[j] = lo_ref[j] * inv
        hi_ref[j] = hi_ref[j] * inv
        return carry

    lax.fori_loop(0, B, finish, 0)


def put_pair(dst, row, first, second):
    low = low_rows()
    for q in range(4):
        f = first[8 * q : 8 * q + 8]
        s = second[8 * q : 8 * q + 8]
        dst[2 * q, row : row + 8] = jnp.where(low, f, swap(s))
        dst[2 * q + 1, row : row + 8] = jnp.where(low, swap(f), s)


def get_pair(src):
    low = low_rows()
    first, second = [], []
    for q in range(4):
        t0 = src[2 * q]
        t1 = src[2 * q + 1]
        first.append(jnp.where(low, t0, swap(t1)))
        second.append(jnp.where(low, swap(t0), t1))
    return jnp.concatenate(first, axis=0), jnp.concatenate(second, axis=0)


def owner_matrix(n, prm, m_ref, y_ref, rf_ref, rb_ref):
    low = low_rows()
    zero = jnp.zeros((8, X), jnp.float32)

    def block(i):
        c = prm[i, 8:16]
        return prm[i, 0:8], jnp.where(low, c, swap(c))

    y_ref[0] = zero
    y_ref[n] = zero
    r0 = prm[0, 0:8]
    rb0 = prm[n - 1, 0:8]
    rf_ref[0] = r0
    rb_ref[n - 1] = rb0
    m_ref[0] = zero
    m_ref[n - 1] = zero

    def step(s, carry):
        r, rb = carry
        z, zt = block(s)
        t = zt / (r + swap(z))
        r = z - zt * t
        rf_ref[s] = r
        i = n - 1 - s
        zb, ztb = block(i)
        tb = ztb / (rb + swap(zb))
        rb = zb - ztb * tb
        rb_ref[i] = rb
        m_ref[s] = jnp.where(low, m_ref[s], t)
        m_ref[i] = jnp.where(low, tb, m_ref[i])
        return r, rb

    def clear(s, carry):
        m_ref[s] = zero
        return carry

    lax.fori_loop(0, n, clear, 0)
    lax.fori_loop(1, n, step, (r0, rb0))

    def admit(i, carry):
        y_ref[i] = 1.0 / (swap(rf_ref[i - 1]) + rb_ref[i])
        return carry

    lax.fori_loop(1, n, admit, 0)


def owner_scan(n, g_ref, m_ref, u_ref, v_ref):
    zero = jnp.zeros((8, X), jnp.float32)
    u_ref[0] = zero
    v_ref[n] = zero

    def step(s, carry):
        u, v = carry
        g = g_ref[s]
        m = m_ref[s]
        u = g - m * swap(g) + m * u
        u_ref[s + 1] = u
        i = n - 1 - s
        gb = g_ref[i]
        mb = m_ref[i]
        v = gb - mb * swap(gb) + mb * v
        v_ref[i] = v
        return u, v

    lax.fori_loop(0, n, step, (zero, zero))


def owner_result(b, u_ref, v_ref, y_ref):
    low = low_rows()
    here = (swap(u_ref[b]) - v_ref[b]) * y_ref[b]
    after = (swap(u_ref[b + 1]) - v_ref[b + 1]) * y_ref[b + 1]
    return jnp.where(low, here, -swap(after))


def local_scan(r_ref, a_ref, b_ref, f_ref, g_ref, inv_ref):
    r0 = r_ref[0]
    rb0 = r_ref[B - 1]
    f_ref[0] = r0
    g_ref[B - 1] = jnp.zeros_like(r0)

    def step(s, carry):
        f, g = carry
        t = B - 1 - s
        f = r_ref[s] + a_ref[s] * f
        bg = b_ref[t] * g
        g = r_ref[t] + bg
        f_ref[s] = f
        g_ref[t] = bg
        return f, g

    f, g = lax.fori_loop(1, B, step, (r0, rb0))
    return g * inv_ref[0], f * inv_ref[B - 1]


def kernel(nz, ny, *refs):
    (c_hbm, v_hbm, w_hbm, k_hbm, o_hbm,
     ca, cb, vv, ww, kz, ky, k0, cym, cyp, czm, czp,
     ay, by, iy, ly, hy, az, bz, iz, lz, hz, tmp, rr, ff, gg, uz, out,
     psy, psz, pry, prz, gsy, gsz, gry, grz,
     my, yy, uy, vy, mz, yz, uo, vo, rf, rb,
     rsy, rsz, rety, retz,
     kye, kze, lsem, hsend, hrecv, psem, grsem, rtsem, ksem, ysem, zsem) = refs
    p = lax.axis_index("gz")
    g = lax.axis_index("gy")

    def zi(k):
        return lax.rem(p + k + nz, nz)

    def yi(k):
        return lax.rem(g + k + ny, ny)

    bar = pltpu.get_barrier_semaphore()
    neighbours = [(dz, dy) for dz in (1, 0, -1) for dy in (1, 0, -1) if dz or dy]
    for dz, dy in neighbours:
        pl.semaphore_signal(bar, inc=1, device_id=(zi(dz), yi(dy)), device_id_type=MESH)

    def greet(r):
        d = 1 << r
        if 2 * d < ny:
            for k in (d, -d):
                pl.semaphore_signal(ysem.at[r], inc=1, device_id=(p, yi(k)), device_id_type=MESH)
        if 2 * d < nz:
            for k in (d, -d):
                pl.semaphore_signal(zsem.at[r], inc=1, device_id=(zi(k), g), device_id_type=MESH)

    def greeted(r):
        if 2 << r < ny:
            pl.semaphore_wait(ysem.at[r], 2)
        if 2 << r < nz:
            pl.semaphore_wait(zsem.at[r], 2)

    loads = [
        pltpu.make_async_copy(k_hbm, kz, lsem.at[0]),
        pltpu.make_async_copy(c_hbm, ca.at[HZ : HZ + B, HY : HY + B], lsem.at[1]),
        pltpu.make_async_copy(v_hbm, vv.at[HZ : HZ + B, HY : HY + B], lsem.at[2]),
        pltpu.make_async_copy(w_hbm, ww.at[HZ : HZ + B, HY : HY + B], lsem.at[3]),
    ]
    for ld in loads:
        ld.start()

    pl.semaphore_wait(bar, len(neighbours))

    def near(d, size, pad, width):
        if d == 0:
            return slice(0, size), slice(pad, pad + size)
        if d > 0:
            return slice(size - width, size), slice(pad - width, pad)
        return slice(0, width), slice(pad + size, pad + size + width)

    halo = []
    for dz, dy in ((0, 1), (0, -1), (1, 0), (-1, 0), (1, 1), (1, -1), (-1, 1), (-1, -1)):
        for src, dst, wz, wy in ((c_hbm, ca, 4, 4), (v_hbm, vv, 3, 4), (w_hbm, ww, 4, 3)):
            if dz and dy:
                wz, wy = 3, 3
            zs, zd = near(dz, B, HZ, wz)
            ys, yd = near(dy, B, HY, wy)
            i = len(halo)
            halo.append(pltpu.make_async_remote_copy(
                src.at[zs, ys], dst.at[zd, yd], hsend.at[i], hrecv.at[i],
                device_id=(zi(dz), yi(dy)), device_id_type=MESH))
    edges = [
        pltpu.make_async_remote_copy(
            k_hbm.at[:, B - 1 : B], kye.at[:, 0:1], ksem.at[0], ksem.at[1],
            device_id=(p, yi(1)), device_id_type=MESH),
        pltpu.make_async_remote_copy(
            k_hbm.at[B - 1], kze, ksem.at[2], ksem.at[3],
            device_id=(zi(1), g), device_id_type=MESH),
    ]
    for h in edges + halo:
        h.start()
    greet(0)

    loads[0].wait()
    kflat = kz.reshape(B * B, X)

    def turn(j, carry):
        ky[j] = kflat[pl.ds(j, B, stride=B), :]
        return carry

    lax.fori_loop(0, B, turn, 0)
    yfirst = jnp.where(g == 0, RATE, 0.0).astype(jnp.float32)
    ylast = jnp.where(g == ny - 1, RATE, 0.0).astype(jnp.float32)
    zfirst = jnp.where(p == 0, RATE, 0.0).astype(jnp.float32)
    zlast = jnp.where(p == nz - 1, RATE, 0.0).astype(jnp.float32)

    greeted(0)
    greet(1)
    factor(ky, yfirst, ylast, ay, by, iy, ly, hy, tmp)
    edges[0].wait_recv()
    below = kye.reshape(B * 8, X)[pl.ds(0, B, stride=8), :]
    put_pair(psy, 0, ly[0] + 1.0 / (HALF_RATE * (below + ky[0])), hy[B - 1])
    put_pair(psy, 8, hy[0], hy[0])
    pry[g] = psy[lax.rem(g, C)]

    def to_y(src, dst, sem, k):
        return pltpu.make_async_remote_copy(
            src.at[lax.rem(g + k, C)], dst.at[g], sem.at[0], sem.at[1],
            device_id=(p, yi(k)), device_id_type=MESH)

    def to_z(src, dst, sem, k):
        return pltpu.make_async_remote_copy(
            src.at[lax.rem(p + k, C)], dst.at[p], sem.at[0], sem.at[1],
            device_id=(zi(k), g), device_id_type=MESH)

    def wait_all(ref, count, sem):
        part = ref.at[pl.ds(0, count)]
        pltpu.make_async_copy(part, part, sem).wait()

    greeted(1)
    greet(2)
    factor(kz, zfirst, zlast, az, bz, iz, lz, hz, tmp)
    greeted(2)
    greet(3)
    greeted(3)
    for k in range(1, ny):
        to_y(psy.at[:, 0:PR], pry.at[:, 0:PR], psem.at[0], k).start()

    edges[1].wait_recv()
    put_pair(psz, 0, lz[0] + 1.0 / (HALF_RATE * (kze[...] + kz[0])), hz[B - 1])
    put_pair(psz, 8, hz[0], hz[0])
    prz[p] = psz[lax.rem(p, C)]

    for ld in loads[1:]:
        ld.wait()
    for h in halo:
        h.wait_recv()
    for k in range(1, nz):
        to_z(psz.at[:, 0:PR], prz.at[:, 0:PR], psem.at[1], k).start()

    zero3 = jnp.zeros((HZ, B + 2 * HY, X), jnp.float32)
    zero_row = jnp.zeros((HY, X), jnp.float32)

    def zero_y(at):
        def body(z, carry):
            for ref in (ca, vv, ww):
                ref[z, at : at + HY] = zero_row
            return carry

        lax.fori_loop(0, B + 2 * HZ, body, 0)

    @pl.when(p == 0)
    def _():
        for ref in (ca, vv, ww):
            ref[0:HZ] = zero3

    @pl.when(p == nz - 1)
    def _():
        for ref in (ca, vv, ww):
            ref[HZ + B : 2 * HZ + B] = zero3

    @pl.when(g == 0)
    def _():
        zero_y(0)

    @pl.when(g == ny - 1)
    def _():
        zero_y(HY + B)

    LO, N5 = 4, B + 8

    def z_face(a, b):
        f = 0.5 * (a + b)
        return jnp.maximum(f, 0.0), jnp.minimum(f, 0.0)

    def weights(z, carry):
        wc, zm_pos, zm_neg = carry
        wp = ww[z + 1, LO : LO + N5]
        zp_pos, zp_neg = z_face(wc, wp)
        vc = vv[z, LO : LO + N5]
        ym_pos, ym_neg = z_face(vv[z, LO - 1 : LO - 1 + N5], vc)
        yp_pos, yp_neg = z_face(vc, vv[z, LO + 1 : LO + 1 + N5])
        cyp[z] = yp_neg
        cym[z] = ym_pos
        czp[z] = zp_neg
        czm[z] = zm_pos
        k0[z] = ((1.0 - yp_pos) + (ym_neg - zp_pos)) + zm_neg
        return wp, zp_pos, zp_neg

    w1 = ww[1, LO : LO + N5]
    lax.fori_loop(1, B + 2 * HZ - 1, weights, (w1, *z_face(ww[0, LO : LO + N5], w1)), unroll=2)

    wrefs = (k0, cym, cyp, czm, czp)
    zero_w = jnp.zeros((HZ - 1, N5, X), jnp.float32)

    def zero_wy(at):
        def body(z, carry):
            for ref in wrefs:
                ref[z, at : at + 4] = jnp.zeros((4, X), jnp.float32)
            return carry

        lax.fori_loop(1, B + 2 * HZ - 1, body, 0)

    @pl.when(p == 0)
    def _():
        for ref in wrefs:
            ref[1:HZ] = zero_w

    @pl.when(p == nz - 1)
    def _():
        for ref in wrefs:
            ref[HZ + B : 2 * HZ + B - 1] = zero_w

    @pl.when(g == 0)
    def _():
        zero_wy(0)

    @pl.when(g == ny - 1)
    def _():
        zero_wy(4 + B)

    for s in range(1, NSUB):
        src, dst = (ca, cb) if s % 2 == 1 else (cb, ca)

        def sub(z, carry, src=src, dst=dst):
            new = ((k0[z] * src[z, LO : LO + N5]
                    + cym[z] * src[z, LO - 1 : LO - 1 + N5])
                   - (cyp[z] * src[z, LO + 1 : LO + 1 + N5]
                      - czm[z] * src[z - 1, LO : LO + N5])
                   - czp[z] * src[z + 1, LO : LO + N5])
            dst[z, LO : LO + N5] = new
            return carry

        lax.fori_loop(s, B + 2 * HZ - s, sub, 0)

    src = cb if NSUB % 2 == 0 else ca
    rflat = rr.reshape(B * B, X)

    def last(z, carry):
        at, up = slice(HY, HY + B), slice(4, 4 + B)
        new = ((k0[z, up] * src[z, at]
                + cym[z, up] * src[z, HY - 1 : HY - 1 + B])
               - (cyp[z, up] * src[z, HY + 1 : HY + 1 + B]
                  - czm[z, up] * src[z - 1, at])
               - czp[z, up] * src[z + 1, at])
        rflat[pl.ds(z - HZ, B, stride=B), :] = new
        return carry

    lax.fori_loop(HZ, HZ + B, last, 0)

    g0, gl = local_scan(rr, ay, by, ff, gg, iy)
    put_pair(gsy, 0, g0, gl)
    gry[g] = gsy[lax.rem(g, C)]
    for k in range(1, ny):
        to_y(gsy, gry, grsem.at[0], k).start()

    wait_all(pry.at[:, 0:PR], ny - 1, psem.at[0, 1])
    owner_matrix(ny, pry, my, yy, rf, rb)

    def base(j, carry):
        ff[j] = (ff[j] + gg[j]) * inv_now[j]
        return carry

    inv_now = iy
    lax.fori_loop(0, B, base, 0)

    wait_all(gry, ny - 1, grsem.at[0, 1])
    owner_scan(ny, gry, my, uy, vy)
    yc = lax.rem(g, C)
    yb = g - yc
    rety[yc] = owner_result(g, uy, vy, yy)
    for m in range(1, C):
        b = yb + lax.rem(yc + m, C)
        rsy[m] = owner_result(b, uy, vy, yy)
        pltpu.make_async_remote_copy(
            rsy.at[m], rety.at[yc], rtsem.at[0, 0], rtsem.at[0, 1],
            device_id=(p, b), device_id_type=MESH).start()

    wait_all(prz.at[:, 0:PR], nz - 1, psem.at[1, 1])
    owner_matrix(nz, prz, mz, yz, rf, rb)

    wait_all(rety, C - 1, rtsem.at[0, 1])
    flo, fhi = get_pair(rety)
    uflat = uz.reshape(B * B, X)

    def end_y(j, carry):
        uflat[pl.ds(j, B, stride=B), :] = ff[j] + flo * ly[j] + fhi * hy[j]
        return carry

    lax.fori_loop(0, B, end_y, 0)

    g0, gl = local_scan(uz, az, bz, ff, gg, iz)
    put_pair(gsz, 0, g0, gl)
    grz[p] = gsz[lax.rem(p, C)]
    for k in range(1, nz):
        to_z(gsz, grz, grsem.at[1], k).start()
    inv_now = iz

    def base_z(j, carry):
        ff[j] = (ff[j] + gg[j]) * iz[j]
        return carry

    lax.fori_loop(0, B, base_z, 0)
    wait_all(grz, nz - 1, grsem.at[1, 1])
    owner_scan(nz, grz, mz, uo, vo)
    zc = lax.rem(p, C)
    retz[zc] = owner_result(p, uo, vo, yz)
    others = [o for o in range(-(C // 2), C // 2) if o != 0]
    for m, o in enumerate(others):
        b = zi(o)
        rsz[m] = owner_result(b, uo, vo, yz)
        pltpu.make_async_remote_copy(
            rsz.at[m], retz.at[zc], rtsem.at[1, 0], rtsem.at[1, 1],
            device_id=(b, g), device_id_type=MESH).start()
    wait_all(retz, C - 1, rtsem.at[1, 1])
    flo, fhi = get_pair(retz)

    def end_z(j, carry):
        out[j] = ff[j] + flo * lz[j] + fhi * hz[j]
        return carry

    stores = []
    for j in range(0, B, OUT):
        lax.fori_loop(j, j + OUT, end_z, 0)
        st = pltpu.make_async_copy(
            out.at[j : j + OUT], o_hbm.at[j : j + OUT], lsem.at[4 + j // OUT])
        st.start()
        stores.append(st)
    for h in edges + halo:
        h.wait_send()
    wait_all(pry.at[:, 0:PR], ny - 1, psem.at[0, 0])
    wait_all(prz.at[:, 0:PR], nz - 1, psem.at[1, 0])
    wait_all(gry, ny - 1, grsem.at[0, 0])
    wait_all(grz, nz - 1, grsem.at[1, 0])
    wait_all(rety, C - 1, rtsem.at[0, 0])
    wait_all(retz, C - 1, rtsem.at[1, 0])
    for st in stores:
        st.wait()


def local(nz, ny, tracer, y_speed, z_speed, kappa):
    f32 = jnp.float32
    pad = pltpu.VMEM((B + 2 * HZ, B + 2 * HY, X), f32)
    blk = pltpu.VMEM((B, B, X), f32)
    wgt = pltpu.VMEM((B + 2 * HZ, B + 8, X), f32)

    def tiles(n, rows=8):
        return pltpu.VMEM((n, rows, X), f32)

    scratch = (
        [pad] * 4 + [blk] * 2 + [wgt] * 5
        + [blk] * 5 + [blk] * 5 + [blk] * 6
        + [tiles(C, 16), tiles(C, 16), tiles(ny, 16), tiles(nz, 16)]
        + [tiles(C), tiles(C), tiles(ny), tiles(nz)]
        + [tiles(ny), tiles(ny + 1), tiles(ny + 1), tiles(ny + 1)]
        + [tiles(nz), tiles(nz + 1), tiles(nz + 1), tiles(nz + 1)]
        + [tiles(ny), tiles(ny)]
        + [tiles(C), tiles(C), tiles(C), tiles(C)]
        + [tiles(B), pltpu.VMEM((B, X), f32), pltpu.SemaphoreType.DMA((4 + B // OUT,)), pltpu.SemaphoreType.DMA((24,)),
           pltpu.SemaphoreType.DMA((24,)), pltpu.SemaphoreType.DMA((2, 2)),
           pltpu.SemaphoreType.DMA((2, 2)), pltpu.SemaphoreType.DMA((2, 2)),
           pltpu.SemaphoreType.DMA((4,)),
           pltpu.SemaphoreType.REGULAR((4,)), pltpu.SemaphoreType.REGULAR((4,))]
    )
    return pl.pallas_call(
        functools.partial(kernel, nz, ny),
        out_shape=jax.ShapeDtypeStruct(tracer.shape, f32),
        in_specs=[pl.BlockSpec(memory_space=pl.ANY)] * 4,
        out_specs=pl.BlockSpec(memory_space=pl.ANY),
        scratch_shapes=scratch,
        compiler_params=pltpu.CompilerParams(
            collective_id=0, has_side_effects=True, vmem_limit_bytes=56000000),
    )(tracer, y_speed, z_speed, kappa)


def solution(mesh):
    nz, ny = mesh.shape["gz"], mesh.shape["gy"]
    return jax.shard_map(
        functools.partial(local, nz, ny),
        mesh=mesh,
        in_specs=(P("gz", "gy", None),) * 4,
        out_specs=P("gz", "gy", None),
        check_vma=False,
    )
```

```python
import functools

import jax
import jax.numpy as jnp
from jax import lax
from jax.experimental import pallas as pl
from jax.experimental.pallas import tpu as pltpu
from jax.sharding import PartitionSpec as P

NSUB = 4
RATE = 500.0
HALF_RATE = 250.0
B = 32
X = 128
HZ = 4
HY = 8
C = 8
PR = 12
OUT = 8
MESH = pl.DeviceIdType.MESH


def low_rows():
    return lax.broadcasted_iota(jnp.int32, (8, X), 0) < 4


def swap(t):
    return pltpu.roll(t, 4, 0)


def factor(kap, first, last, a_ref, b_ref, inv_ref, lo_ref, hi_ref, tmp_ref):
    e0 = 1.0 + first * kap[0]
    b0 = 1.0 + last * kap[B - 1]
    one = jnp.ones_like(e0)
    inv_ref[0] = e0
    lo_ref[0] = one
    tmp_ref[B - 1] = b0
    hi_ref[B - 1] = one

    def step(s, carry):
        e, eb, ac, bc, kf, kb = carry
        t = B - 1 - s
        kn = kap[s]
        kp = kap[t]
        face = HALF_RATE * (kf + kn)
        a = face / (e + face)
        e = 1.0 + a * e
        ac = ac * a
        faceb = HALF_RATE * (kb + kp)
        b = faceb / (eb + faceb)
        eb = 1.0 + b * eb
        bc = bc * b
        a_ref[s] = a
        inv_ref[s] = e
        lo_ref[s] = ac
        b_ref[t] = b
        tmp_ref[t] = eb
        hi_ref[t] = bc
        return e, eb, ac, bc, kn, kp

    lax.fori_loop(1, B, step, (e0, b0, one, one, kap[0], kap[B - 1]))

    def finish(j, carry):
        inv = 1.0 / (inv_ref[j] + tmp_ref[j] - 1.0)
        inv_ref[j] = inv
        lo_ref[j] = lo_ref[j] * inv
        hi_ref[j] = hi_ref[j] * inv
        return carry

    lax.fori_loop(0, B, finish, 0)


def put_pair(dst, row, first, second):
    low = low_rows()
    for q in range(4):
        f = first[8 * q : 8 * q + 8]
        s = second[8 * q : 8 * q + 8]
        dst[2 * q, row : row + 8] = jnp.where(low, f, swap(s))
        dst[2 * q + 1, row : row + 8] = jnp.where(low, swap(f), s)


def get_pair(src):
    low = low_rows()
    first, second = [], []
    for q in range(4):
        t0 = src[2 * q]
        t1 = src[2 * q + 1]
        first.append(jnp.where(low, t0, swap(t1)))
        second.append(jnp.where(low, swap(t0), t1))
    return jnp.concatenate(first, axis=0), jnp.concatenate(second, axis=0)


def owner_matrix(n, prm, m_ref, y_ref, rf_ref, rb_ref):
    low = low_rows()
    zero = jnp.zeros((8, X), jnp.float32)

    def block(i):
        c = prm[i, 8:16]
        return prm[i, 0:8], jnp.where(low, c, swap(c))

    y_ref[0] = zero
    y_ref[n] = zero
    r0 = prm[0, 0:8]
    rb0 = prm[n - 1, 0:8]
    rf_ref[0] = r0
    rb_ref[n - 1] = rb0
    m_ref[0] = zero
    m_ref[n - 1] = zero

    def step(s, carry):
        r, rb = carry
        z, zt = block(s)
        t = zt / (r + swap(z))
        r = z - zt * t
        rf_ref[s] = r
        i = n - 1 - s
        zb, ztb = block(i)
        tb = ztb / (rb + swap(zb))
        rb = zb - ztb * tb
        rb_ref[i] = rb
        m_ref[s] = jnp.where(low, m_ref[s], t)
        m_ref[i] = jnp.where(low, tb, m_ref[i])
        return r, rb

    def clear(s, carry):
        m_ref[s] = zero
        return carry

    lax.fori_loop(0, n, clear, 0)
    lax.fori_loop(1, n, step, (r0, rb0))

    def admit(i, carry):
        y_ref[i] = 1.0 / (swap(rf_ref[i - 1]) + rb_ref[i])
        return carry

    lax.fori_loop(1, n, admit, 0)


def owner_scan(n, g_ref, m_ref, u_ref, v_ref):
    zero = jnp.zeros((8, X), jnp.float32)
    u_ref[0] = zero
    v_ref[n] = zero

    def step(s, carry):
        u, v = carry
        g = g_ref[s]
        m = m_ref[s]
        u = g - m * swap(g) + m * u
        u_ref[s + 1] = u
        i = n - 1 - s
        gb = g_ref[i]
        mb = m_ref[i]
        v = gb - mb * swap(gb) + mb * v
        v_ref[i] = v
        return u, v

    lax.fori_loop(0, n, step, (zero, zero))


def owner_result(b, u_ref, v_ref, y_ref):
    low = low_rows()
    here = (swap(u_ref[b]) - v_ref[b]) * y_ref[b]
    after = (swap(u_ref[b + 1]) - v_ref[b + 1]) * y_ref[b + 1]
    return jnp.where(low, here, -swap(after))


def local_scan(r_ref, a_ref, b_ref, f_ref, g_ref, inv_ref):
    r0 = r_ref[0]
    rb0 = r_ref[B - 1]
    f_ref[0] = r0
    g_ref[B - 1] = jnp.zeros_like(r0)

    def step(s, carry):
        f, g = carry
        t = B - 1 - s
        f = r_ref[s] + a_ref[s] * f
        bg = b_ref[t] * g
        g = r_ref[t] + bg
        f_ref[s] = f
        g_ref[t] = bg
        return f, g

    f, g = lax.fori_loop(1, B, step, (r0, rb0))
    return g * inv_ref[0], f * inv_ref[B - 1]


def kernel(nz, ny, *refs):
    (c_hbm, v_hbm, w_hbm, k_hbm, o_hbm,
     ca, cb, vv, ww, kz, ky, k0, cym, cyp, czm, czp,
     ay, by, iy, ly, hy, az, bz, iz, lz, hz, tmp, rr, ff, gg, uz, out,
     psy, psz, pry, prz, gsy, gsz, gry, grz,
     my, yy, uy, vy, mz, yz, uo, vo, rf, rb,
     rsy, rsz, rety, retz,
     kye, kze, lsem, hsend, hrecv, psem, grsem, rtsem, ksem, ysem, zsem) = refs
    p = lax.axis_index("gz")
    g = lax.axis_index("gy")

    def zi(k):
        return lax.rem(p + k + nz, nz)

    def yi(k):
        return lax.rem(g + k + ny, ny)

    bar = pltpu.get_barrier_semaphore()
    neighbours = [(dz, dy) for dz in (1, 0, -1) for dy in (1, 0, -1) if dz or dy]
    for dz, dy in neighbours:
        pl.semaphore_signal(bar, inc=1, device_id=(zi(dz), yi(dy)), device_id_type=MESH)

    def greet(r):
        d = 1 << r
        if 2 * d < ny:
            for k in (d, -d):
                pl.semaphore_signal(ysem.at[r], inc=1, device_id=(p, yi(k)), device_id_type=MESH)
        if 2 * d < nz:
            for k in (d, -d):
                pl.semaphore_signal(zsem.at[r], inc=1, device_id=(zi(k), g), device_id_type=MESH)

    def greeted(r):
        if 2 << r < ny:
            pl.semaphore_wait(ysem.at[r], 2)
        if 2 << r < nz:
            pl.semaphore_wait(zsem.at[r], 2)

    loads = [
        pltpu.make_async_copy(k_hbm, kz, lsem.at[0]),
        pltpu.make_async_copy(c_hbm, ca.at[HZ : HZ + B, HY : HY + B], lsem.at[1]),
        pltpu.make_async_copy(v_hbm, vv.at[HZ : HZ + B, HY : HY + B], lsem.at[2]),
        pltpu.make_async_copy(w_hbm, ww.at[HZ : HZ + B, HY : HY + B], lsem.at[3]),
    ]
    for ld in loads:
        ld.start()

    pl.semaphore_wait(bar, len(neighbours))

    def near(d, size, pad, width):
        if d == 0:
            return slice(0, size), slice(pad, pad + size)
        if d > 0:
            return slice(size - width, size), slice(pad - width, pad)
        return slice(0, width), slice(pad + size, pad + size + width)

    halo = []
    for dz, dy in ((0, 1), (0, -1), (1, 0), (-1, 0), (1, 1), (1, -1), (-1, 1), (-1, -1)):
        for src, dst, wz, wy in ((c_hbm, ca, 4, 4), (v_hbm, vv, 3, 4), (w_hbm, ww, 4, 3)):
            if dz and dy:
                wz, wy = 3, 3
            zs, zd = near(dz, B, HZ, wz)
            ys, yd = near(dy, B, HY, wy)
            i = len(halo)
            halo.append(pltpu.make_async_remote_copy(
                src.at[zs, ys], dst.at[zd, yd], hsend.at[i], hrecv.at[i],
                device_id=(zi(dz), yi(dy)), device_id_type=MESH))
    edges = [
        pltpu.make_async_remote_copy(
            k_hbm.at[:, B - 1 : B], kye.at[:, 0:1], ksem.at[0], ksem.at[1],
            device_id=(p, yi(1)), device_id_type=MESH),
        pltpu.make_async_remote_copy(
            k_hbm.at[B - 1], kze, ksem.at[2], ksem.at[3],
            device_id=(zi(1), g), device_id_type=MESH),
    ]
    for h in edges + halo:
        h.start()
    greet(0)

    loads[0].wait()
    kflat = kz.reshape(B * B, X)

    def turn(j, carry):
        ky[j] = kflat[pl.ds(j, B, stride=B), :]
        return carry

    lax.fori_loop(0, B, turn, 0)
    yfirst = jnp.where(g == 0, RATE, 0.0).astype(jnp.float32)
    ylast = jnp.where(g == ny - 1, RATE, 0.0).astype(jnp.float32)
    zfirst = jnp.where(p == 0, RATE, 0.0).astype(jnp.float32)
    zlast = jnp.where(p == nz - 1, RATE, 0.0).astype(jnp.float32)

    greeted(0)
    greet(1)
    factor(ky, yfirst, ylast, ay, by, iy, ly, hy, tmp)
    greeted(1)
    greet(2)
    edges[0].wait_recv()
    below = kye.reshape(B * 8, X)[pl.ds(0, B, stride=8), :]
    put_pair(psy, 0, ly[0] + 1.0 / (HALF_RATE * (below + ky[0])), hy[B - 1])
    put_pair(psy, 8, hy[0], hy[0])
    pry[g] = psy[lax.rem(g, C)]

    def to_y(src, dst, sem, k):
        return pltpu.make_async_remote_copy(
            src.at[lax.rem(g + k, C)], dst.at[g], sem.at[0], sem.at[1],
            device_id=(p, yi(k)), device_id_type=MESH)

    def to_z(src, dst, sem, k):
        return pltpu.make_async_remote_copy(
            src.at[lax.rem(p + k, C)], dst.at[p], sem.at[0], sem.at[1],
            device_id=(zi(k), g), device_id_type=MESH)

    def wait_all(ref, count, sem):
        part = ref.at[pl.ds(0, count)]
        pltpu.make_async_copy(part, part, sem).wait()

    greeted(2)
    greet(3)
    greeted(3)
    for k in range(1, ny):
        to_y(psy.at[:, 0:PR], pry.at[:, 0:PR], psem.at[0], k).start()


    for ld in loads[1:]:
        ld.wait()
    for h in halo:
        h.wait_recv()

    zero3 = jnp.zeros((HZ, B + 2 * HY, X), jnp.float32)
    zero_row = jnp.zeros((HY, X), jnp.float32)

    def zero_y(at):
        def body(z, carry):
            for ref in (ca, vv, ww):
                ref[z, at : at + HY] = zero_row
            return carry

        lax.fori_loop(0, B + 2 * HZ, body, 0)

    @pl.when(p == 0)
    def _():
        for ref in (ca, vv, ww):
            ref[0:HZ] = zero3

    @pl.when(p == nz - 1)
    def _():
        for ref in (ca, vv, ww):
            ref[HZ + B : 2 * HZ + B] = zero3

    @pl.when(g == 0)
    def _():
        zero_y(0)

    @pl.when(g == ny - 1)
    def _():
        zero_y(HY + B)

    LO, N5 = 4, B + 8

    def z_face(a, b):
        f = 0.5 * (a + b)
        return jnp.maximum(f, 0.0), jnp.minimum(f, 0.0)

    def weights(z, carry):
        wc, zm_pos, zm_neg = carry
        wp = ww[z + 1, LO : LO + N5]
        zp_pos, zp_neg = z_face(wc, wp)
        vc = vv[z, LO : LO + N5]
        ym_pos, ym_neg = z_face(vv[z, LO - 1 : LO - 1 + N5], vc)
        yp_pos, yp_neg = z_face(vc, vv[z, LO + 1 : LO + 1 + N5])
        cyp[z] = yp_neg
        cym[z] = ym_pos
        czp[z] = zp_neg
        czm[z] = zm_pos
        k0[z] = ((1.0 - yp_pos) + (ym_neg - zp_pos)) + zm_neg
        return wp, zp_pos, zp_neg

    w1 = ww[1, LO : LO + N5]
    lax.fori_loop(1, B + 2 * HZ - 1, weights, (w1, *z_face(ww[0, LO : LO + N5], w1)), unroll=2)

    wrefs = (k0, cym, cyp, czm, czp)
    zero_w = jnp.zeros((HZ - 1, N5, X), jnp.float32)

    def zero_wy(at):
        def body(z, carry):
            for ref in wrefs:
                ref[z, at : at + 4] = jnp.zeros((4, X), jnp.float32)
            return carry

        lax.fori_loop(1, B + 2 * HZ - 1, body, 0)

    @pl.when(p == 0)
    def _():
        for ref in wrefs:
            ref[1:HZ] = zero_w

    @pl.when(p == nz - 1)
    def _():
        for ref in wrefs:
            ref[HZ + B : 2 * HZ + B - 1] = zero_w

    @pl.when(g == 0)
    def _():
        zero_wy(0)

    @pl.when(g == ny - 1)
    def _():
        zero_wy(4 + B)

    for s in range(1, NSUB):
        src, dst = (ca, cb) if s % 2 == 1 else (cb, ca)

        def sub(z, carry, src=src, dst=dst):
            new = ((k0[z] * src[z, LO : LO + N5]
                    + cym[z] * src[z, LO - 1 : LO - 1 + N5])
                   - (cyp[z] * src[z, LO + 1 : LO + 1 + N5]
                      - czm[z] * src[z - 1, LO : LO + N5])
                   - czp[z] * src[z + 1, LO : LO + N5])
            dst[z, LO : LO + N5] = new
            return carry

        lax.fori_loop(s, B + 2 * HZ - s, sub, 0)

    src = cb if NSUB % 2 == 0 else ca
    rflat = rr.reshape(B * B, X)

    def last(z, carry):
        at, up = slice(HY, HY + B), slice(4, 4 + B)
        new = ((k0[z, up] * src[z, at]
                + cym[z, up] * src[z, HY - 1 : HY - 1 + B])
               - (cyp[z, up] * src[z, HY + 1 : HY + 1 + B]
                  - czm[z, up] * src[z - 1, at])
               - czp[z, up] * src[z + 1, at])
        rflat[pl.ds(z - HZ, B, stride=B), :] = new
        return carry

    lax.fori_loop(HZ, HZ + B, last, 0)

    g0, gl = local_scan(rr, ay, by, ff, gg, iy)
    put_pair(gsy, 0, g0, gl)
    gry[g] = gsy[lax.rem(g, C)]
    for k in range(1, ny):
        to_y(gsy, gry, grsem.at[0], k).start()

    factor(kz, zfirst, zlast, az, bz, iz, lz, hz, tmp)
    edges[1].wait_recv()
    put_pair(psz, 0, lz[0] + 1.0 / (HALF_RATE * (kze[...] + kz[0])), hz[B - 1])
    put_pair(psz, 8, hz[0], hz[0])
    prz[p] = psz[lax.rem(p, C)]
    for k in range(1, nz):
        to_z(psz.at[:, 0:PR], prz.at[:, 0:PR], psem.at[1], k).start()

    wait_all(pry.at[:, 0:PR], ny - 1, psem.at[0, 1])
    owner_matrix(ny, pry, my, yy, rf, rb)

    wait_all(gry, ny - 1, grsem.at[0, 1])
    owner_scan(ny, gry, my, uy, vy)
    yc = lax.rem(g, C)
    yb = g - yc
    rety[yc] = owner_result(g, uy, vy, yy)
    for m in range(1, C):
        b = yb + lax.rem(yc + m, C)
        rsy[m] = owner_result(b, uy, vy, yy)
        pltpu.make_async_remote_copy(
            rsy.at[m], rety.at[yc], rtsem.at[0, 0], rtsem.at[0, 1],
            device_id=(p, b), device_id_type=MESH).start()

    def base(j, carry):
        ff[j] = (ff[j] + gg[j]) * iy[j]
        return carry

    lax.fori_loop(0, B, base, 0)

    wait_all(rety, C - 1, rtsem.at[0, 1])
    flo, fhi = get_pair(rety)
    uflat = uz.reshape(B * B, X)

    def end_y(j, carry):
        uflat[pl.ds(j, B, stride=B), :] = ff[j] + flo * ly[j] + fhi * hy[j]
        return carry

    lax.fori_loop(0, B, end_y, 0)

    g0, gl = local_scan(uz, az, bz, ff, gg, iz)
    put_pair(gsz, 0, g0, gl)
    grz[p] = gsz[lax.rem(p, C)]
    for k in range(1, nz):
        to_z(gsz, grz, grsem.at[1], k).start()

    def base_z(j, carry):
        ff[j] = (ff[j] + gg[j]) * iz[j]
        return carry

    lax.fori_loop(0, B, base_z, 0)
    wait_all(prz.at[:, 0:PR], nz - 1, psem.at[1, 1])
    owner_matrix(nz, prz, mz, yz, rf, rb)

    wait_all(grz, nz - 1, grsem.at[1, 1])
    owner_scan(nz, grz, mz, uo, vo)
    zc = lax.rem(p, C)
    retz[zc] = owner_result(p, uo, vo, yz)
    others = [o for o in range(-(C // 2), C // 2) if o != 0]
    for m, o in enumerate(others):
        b = zi(o)
        rsz[m] = owner_result(b, uo, vo, yz)
        pltpu.make_async_remote_copy(
            rsz.at[m], retz.at[zc], rtsem.at[1, 0], rtsem.at[1, 1],
            device_id=(b, g), device_id_type=MESH).start()
    wait_all(retz, C - 1, rtsem.at[1, 1])
    flo, fhi = get_pair(retz)

    def end_z(j, carry):
        out[j] = ff[j] + flo * lz[j] + fhi * hz[j]
        return carry

    stores = []
    for j in range(0, B, OUT):
        lax.fori_loop(j, j + OUT, end_z, 0)
        st = pltpu.make_async_copy(
            out.at[j : j + OUT], o_hbm.at[j : j + OUT], lsem.at[4 + j // OUT])
        st.start()
        stores.append(st)
    for h in edges + halo:
        h.wait_send()
    wait_all(pry.at[:, 0:PR], ny - 1, psem.at[0, 0])
    wait_all(prz.at[:, 0:PR], nz - 1, psem.at[1, 0])
    wait_all(gry, ny - 1, grsem.at[0, 0])
    wait_all(grz, nz - 1, grsem.at[1, 0])
    wait_all(rety, C - 1, rtsem.at[0, 0])
    wait_all(retz, C - 1, rtsem.at[1, 0])
    for st in stores:
        st.wait()


def local(nz, ny, tracer, y_speed, z_speed, kappa):
    f32 = jnp.float32
    pad = pltpu.VMEM((B + 2 * HZ, B + 2 * HY, X), f32)
    blk = pltpu.VMEM((B, B, X), f32)
    wgt = pltpu.VMEM((B + 2 * HZ, B + 8, X), f32)

    def tiles(n, rows=8):
        return pltpu.VMEM((n, rows, X), f32)

    scratch = (
        [pad] * 4 + [blk] * 2 + [wgt] * 5
        + [blk] * 5 + [blk] * 5 + [blk] * 6
        + [tiles(C, 16), tiles(C, 16), tiles(ny, 16), tiles(nz, 16)]
        + [tiles(C), tiles(C), tiles(ny), tiles(nz)]
        + [tiles(ny), tiles(ny + 1), tiles(ny + 1), tiles(ny + 1)]
        + [tiles(nz), tiles(nz + 1), tiles(nz + 1), tiles(nz + 1)]
        + [tiles(ny), tiles(ny)]
        + [tiles(C), tiles(C), tiles(C), tiles(C)]
        + [tiles(B), pltpu.VMEM((B, X), f32), pltpu.SemaphoreType.DMA((4 + B // OUT,)), pltpu.SemaphoreType.DMA((24,)),
           pltpu.SemaphoreType.DMA((24,)), pltpu.SemaphoreType.DMA((2, 2)),
           pltpu.SemaphoreType.DMA((2, 2)), pltpu.SemaphoreType.DMA((2, 2)),
           pltpu.SemaphoreType.DMA((4,)),
           pltpu.SemaphoreType.REGULAR((4,)), pltpu.SemaphoreType.REGULAR((4,))]
    )
    return pl.pallas_call(
        functools.partial(kernel, nz, ny),
        out_shape=jax.ShapeDtypeStruct(tracer.shape, f32),
        in_specs=[pl.BlockSpec(memory_space=pl.ANY)] * 4,
        out_specs=pl.BlockSpec(memory_space=pl.ANY),
        scratch_shapes=scratch,
        compiler_params=pltpu.CompilerParams(
            collective_id=0, has_side_effects=True, vmem_limit_bytes=56000000),
    )(tracer, y_speed, z_speed, kappa)


def solution(mesh):
    nz, ny = mesh.shape["gz"], mesh.shape["gy"]
    return jax.shard_map(
        functools.partial(local, nz, ny),
        mesh=mesh,
        in_specs=(P("gz", "gy", None),) * 4,
        out_specs=P("gz", "gy", None),
        check_vma=False,
    )
```

```python
import functools

import jax
import jax.numpy as jnp
from jax import lax
from jax.experimental import pallas as pl
from jax.experimental.pallas import tpu as pltpu
from jax.sharding import PartitionSpec as P

NSUB = 4
RATE = 500.0
HALF_RATE = 250.0
B = 32
X = 128
HZ = 4
HY = 8
C = 8
PR = 12
OUT = 8
MESH = pl.DeviceIdType.MESH


def low_rows():
    return lax.broadcasted_iota(jnp.int32, (8, X), 0) < 4


def swap(t):
    return pltpu.roll(t, 4, 0)


def factor(kap, first, last, a_ref, b_ref, inv_ref, lo_ref, hi_ref, tmp_ref):
    e0 = 1.0 + first * kap[0]
    b0 = 1.0 + last * kap[B - 1]
    one = jnp.ones_like(e0)
    inv_ref[0] = e0
    lo_ref[0] = one
    tmp_ref[B - 1] = b0
    hi_ref[B - 1] = one

    def step(s, carry):
        e, eb, ac, bc, kf, kb = carry
        t = B - 1 - s
        kn = kap[s]
        kp = kap[t]
        face = HALF_RATE * (kf + kn)
        a = face / (e + face)
        e = 1.0 + a * e
        ac = ac * a
        faceb = HALF_RATE * (kb + kp)
        b = faceb / (eb + faceb)
        eb = 1.0 + b * eb
        bc = bc * b
        a_ref[s] = a
        inv_ref[s] = e
        lo_ref[s] = ac
        b_ref[t] = b
        tmp_ref[t] = eb
        hi_ref[t] = bc
        return e, eb, ac, bc, kn, kp

    lax.fori_loop(1, B, step, (e0, b0, one, one, kap[0], kap[B - 1]))

    def finish(j, carry):
        inv = 1.0 / (inv_ref[j] + tmp_ref[j] - 1.0)
        inv_ref[j] = inv
        lo_ref[j] = lo_ref[j] * inv
        hi_ref[j] = hi_ref[j] * inv
        return carry

    lax.fori_loop(0, B, finish, 0)


def put_pair(dst, row, first, second):
    low = low_rows()
    for q in range(4):
        f = first[8 * q : 8 * q + 8]
        s = second[8 * q : 8 * q + 8]
        dst[2 * q, row : row + 8] = jnp.where(low, f, swap(s))
        dst[2 * q + 1, row : row + 8] = jnp.where(low, swap(f), s)


def get_pair(src):
    low = low_rows()
    first, second = [], []
    for q in range(4):
        t0 = src[2 * q]
        t1 = src[2 * q + 1]
        first.append(jnp.where(low, t0, swap(t1)))
        second.append(jnp.where(low, swap(t0), t1))
    return jnp.concatenate(first, axis=0), jnp.concatenate(second, axis=0)


def owner_matrix(n, prm, m_ref, y_ref, rf_ref, rb_ref):
    low = low_rows()
    zero = jnp.zeros((8, X), jnp.float32)

    def block(i):
        c = prm[i, 8:16]
        return prm[i, 0:8], jnp.where(low, c, swap(c))

    y_ref[0] = zero
    y_ref[n] = zero
    r0 = prm[0, 0:8]
    rb0 = prm[n - 1, 0:8]
    rf_ref[0] = r0
    rb_ref[n - 1] = rb0
    m_ref[0] = zero
    m_ref[n - 1] = zero

    def step(s, carry):
        r, rb = carry
        z, zt = block(s)
        t = zt / (r + swap(z))
        r = z - zt * t
        rf_ref[s] = r
        i = n - 1 - s
        zb, ztb = block(i)
        tb = ztb / (rb + swap(zb))
        rb = zb - ztb * tb
        rb_ref[i] = rb
        m_ref[s] = jnp.where(low, m_ref[s], t)
        m_ref[i] = jnp.where(low, tb, m_ref[i])
        return r, rb

    def clear(s, carry):
        m_ref[s] = zero
        return carry

    lax.fori_loop(0, n, clear, 0)
    lax.fori_loop(1, n, step, (r0, rb0))

    def admit(i, carry):
        y_ref[i] = 1.0 / (swap(rf_ref[i - 1]) + rb_ref[i])
        return carry

    lax.fori_loop(1, n, admit, 0)


def owner_scan(n, g_ref, m_ref, u_ref, v_ref):
    zero = jnp.zeros((8, X), jnp.float32)
    u_ref[0] = zero
    v_ref[n] = zero

    def step(s, carry):
        u, v = carry
        g = g_ref[s]
        m = m_ref[s]
        u = g - m * swap(g) + m * u
        u_ref[s + 1] = u
        i = n - 1 - s
        gb = g_ref[i]
        mb = m_ref[i]
        v = gb - mb * swap(gb) + mb * v
        v_ref[i] = v
        return u, v

    lax.fori_loop(0, n, step, (zero, zero))


def owner_result(b, u_ref, v_ref, y_ref):
    low = low_rows()
    here = (swap(u_ref[b]) - v_ref[b]) * y_ref[b]
    after = (swap(u_ref[b + 1]) - v_ref[b + 1]) * y_ref[b + 1]
    return jnp.where(low, here, -swap(after))


def local_scan(r_ref, a_ref, b_ref, f_ref, g_ref, inv_ref):
    r0 = r_ref[0]
    rb0 = r_ref[B - 1]
    f_ref[0] = r0
    g_ref[B - 1] = jnp.zeros_like(r0)

    def step(s, carry):
        f, g = carry
        t = B - 1 - s
        f = r_ref[s] + a_ref[s] * f
        bg = b_ref[t] * g
        g = r_ref[t] + bg
        f_ref[s] = f
        g_ref[t] = bg
        return f, g

    f, g = lax.fori_loop(1, B, step, (r0, rb0))
    return g * inv_ref[0], f * inv_ref[B - 1]


def kernel(nz, ny, *refs):
    (c_hbm, v_hbm, w_hbm, k_hbm, o_hbm,
     ca, cb, vv, ww, kz, ky, k0, cym, cyp, czm, czp,
     ay, by, iy, ly, hy, az, bz, iz, lz, hz, tmp, rr, ff, gg, uz, out,
     psy, psz, pry, prz, gsy, gsz, gry, grz,
     my, yy, uy, vy, mz, yz, uo, vo, rf, rb,
     rsy, rsz, rety, retz,
     kye, kze, lsem, hsend, hrecv, psem, grsem, rtsem, ksem, ysem, zsem) = refs
    p = lax.axis_index("gz")
    g = lax.axis_index("gy")

    def zi(k):
        return lax.rem(p + k + nz, nz)

    def yi(k):
        return lax.rem(g + k + ny, ny)

    bar = pltpu.get_barrier_semaphore()
    neighbours = [(dz, dy) for dz in (1, 0, -1) for dy in (1, 0, -1) if dz or dy]
    for dz, dy in neighbours:
        pl.semaphore_signal(bar, inc=1, device_id=(zi(dz), yi(dy)), device_id_type=MESH)

    def greet(r):
        d = 1 << r
        if 2 * d < ny:
            for k in (d, -d):
                pl.semaphore_signal(ysem.at[r], inc=1, device_id=(p, yi(k)), device_id_type=MESH)
        if 2 * d < nz:
            for k in (d, -d):
                pl.semaphore_signal(zsem.at[r], inc=1, device_id=(zi(k), g), device_id_type=MESH)

    def greeted(r):
        if 2 << r < ny:
            pl.semaphore_wait(ysem.at[r], 2)
        if 2 << r < nz:
            pl.semaphore_wait(zsem.at[r], 2)

    loads = [
        pltpu.make_async_copy(k_hbm, kz, lsem.at[0]),
        pltpu.make_async_copy(c_hbm, ca.at[HZ : HZ + B, HY : HY + B], lsem.at[1]),
        pltpu.make_async_copy(v_hbm, vv.at[HZ : HZ + B, HY : HY + B], lsem.at[2]),
        pltpu.make_async_copy(w_hbm, ww.at[HZ : HZ + B, HY : HY + B], lsem.at[3]),
    ]
    for ld in loads:
        ld.start()

    pl.semaphore_wait(bar, len(neighbours))

    def near(d, size, pad, width):
        if d == 0:
            return slice(0, size), slice(pad, pad + size)
        if d > 0:
            return slice(size - width, size), slice(pad - width, pad)
        return slice(0, width), slice(pad + size, pad + size + width)

    halo = []
    for dz, dy in ((1, 1), (1, -1), (-1, 1), (-1, -1), (0, 1), (0, -1), (1, 0), (-1, 0)):
        for src, dst, wz, wy in ((c_hbm, ca, 4, 4), (v_hbm, vv, 3, 4), (w_hbm, ww, 4, 3)):
            if dz and dy:
                wz, wy = 3, 3
            zs, zd = near(dz, B, HZ, wz)
            ys, yd = near(dy, B, HY, wy)
            i = len(halo)
            halo.append(pltpu.make_async_remote_copy(
                src.at[zs, ys], dst.at[zd, yd], hsend.at[i], hrecv.at[i],
                device_id=(zi(dz), yi(dy)), device_id_type=MESH))
    edges = [
        pltpu.make_async_remote_copy(
            k_hbm.at[:, B - 1 : B], kye.at[:, 0:1], ksem.at[0], ksem.at[1],
            device_id=(p, yi(1)), device_id_type=MESH),
        pltpu.make_async_remote_copy(
            k_hbm.at[B - 1], kze, ksem.at[2], ksem.at[3],
            device_id=(zi(1), g), device_id_type=MESH),
    ]
    for h in edges + halo:
        h.start()
    greet(0)

    loads[0].wait()
    kflat = kz.reshape(B * B, X)

    def turn(j, carry):
        ky[j] = kflat[pl.ds(j, B, stride=B), :]
        return carry

    lax.fori_loop(0, B, turn, 0)
    yfirst = jnp.where(g == 0, RATE, 0.0).astype(jnp.float32)
    ylast = jnp.where(g == ny - 1, RATE, 0.0).astype(jnp.float32)
    zfirst = jnp.where(p == 0, RATE, 0.0).astype(jnp.float32)
    zlast = jnp.where(p == nz - 1, RATE, 0.0).astype(jnp.float32)

    greeted(0)
    greet(1)
    factor(ky, yfirst, ylast, ay, by, iy, ly, hy, tmp)
    greeted(1)
    greet(2)
    edges[0].wait_recv()
    below = kye.reshape(B * 8, X)[pl.ds(0, B, stride=8), :]
    put_pair(psy, 0, ly[0] + 1.0 / (HALF_RATE * (below + ky[0])), hy[B - 1])
    put_pair(psy, 8, hy[0], hy[0])
    pry[g] = psy[lax.rem(g, C)]

    def to_y(src, dst, sem, k):
        return pltpu.make_async_remote_copy(
            src.at[lax.rem(g + k, C)], dst.at[g], sem.at[0], sem.at[1],
            device_id=(p, yi(k)), device_id_type=MESH)

    def to_z(src, dst, sem, k):
        return pltpu.make_async_remote_copy(
            src.at[lax.rem(p + k, C)], dst.at[p], sem.at[0], sem.at[1],
            device_id=(zi(k), g), device_id_type=MESH)

    def wait_all(ref, count, sem):
        part = ref.at[pl.ds(0, count)]
        pltpu.make_async_copy(part, part, sem).wait()

    greeted(2)
    greet(3)
    greeted(3)
    for k in range(1, ny):
        to_y(psy.at[:, 0:PR], pry.at[:, 0:PR], psem.at[0], k).start()


    for ld in loads[1:]:
        ld.wait()
    for h in halo:
        h.wait_recv()

    zero3 = jnp.zeros((HZ, B + 2 * HY, X), jnp.float32)
    zero_row = jnp.zeros((HY, X), jnp.float32)

    def zero_y(at):
        def body(z, carry):
            for ref in (ca, vv, ww):
                ref[z, at : at + HY] = zero_row
            return carry

        lax.fori_loop(0, B + 2 * HZ, body, 0)

    @pl.when(p == 0)
    def _():
        for ref in (ca, vv, ww):
            ref[0:HZ] = zero3

    @pl.when(p == nz - 1)
    def _():
        for ref in (ca, vv, ww):
            ref[HZ + B : 2 * HZ + B] = zero3

    @pl.when(g == 0)
    def _():
        zero_y(0)

    @pl.when(g == ny - 1)
    def _():
        zero_y(HY + B)

    LO, N5 = 4, B + 8

    def z_face(a, b):
        f = 0.5 * (a + b)
        return jnp.maximum(f, 0.0), jnp.minimum(f, 0.0)

    def weights(z, carry):
        wc, zm_pos, zm_neg = carry
        wp = ww[z + 1, LO : LO + N5]
        zp_pos, zp_neg = z_face(wc, wp)
        vc = vv[z, LO : LO + N5]
        ym_pos, ym_neg = z_face(vv[z, LO - 1 : LO - 1 + N5], vc)
        yp_pos, yp_neg = z_face(vc, vv[z, LO + 1 : LO + 1 + N5])
        cyp[z] = yp_neg
        cym[z] = ym_pos
        czp[z] = zp_neg
        czm[z] = zm_pos
        k0[z] = ((1.0 - yp_pos) + (ym_neg - zp_pos)) + zm_neg
        return wp, zp_pos, zp_neg

    w1 = ww[1, LO : LO + N5]
    lax.fori_loop(1, B + 2 * HZ - 1, weights, (w1, *z_face(ww[0, LO : LO + N5], w1)), unroll=2)

    wrefs = (k0, cym, cyp, czm, czp)
    zero_w = jnp.zeros((HZ - 1, N5, X), jnp.float32)

    def zero_wy(at):
        def body(z, carry):
            for ref in wrefs:
                ref[z, at : at + 4] = jnp.zeros((4, X), jnp.float32)
            return carry

        lax.fori_loop(1, B + 2 * HZ - 1, body, 0)

    @pl.when(p == 0)
    def _():
        for ref in wrefs:
            ref[1:HZ] = zero_w

    @pl.when(p == nz - 1)
    def _():
        for ref in wrefs:
            ref[HZ + B : 2 * HZ + B - 1] = zero_w

    @pl.when(g == 0)
    def _():
        zero_wy(0)

    @pl.when(g == ny - 1)
    def _():
        zero_wy(4 + B)

    for s in range(1, NSUB):
        src, dst = (ca, cb) if s % 2 == 1 else (cb, ca)

        def sub(z, carry, src=src, dst=dst):
            new = ((k0[z] * src[z, LO : LO + N5]
                    + cym[z] * src[z, LO - 1 : LO - 1 + N5])
                   - (cyp[z] * src[z, LO + 1 : LO + 1 + N5]
                      - czm[z] * src[z - 1, LO : LO + N5])
                   - czp[z] * src[z + 1, LO : LO + N5])
            dst[z, LO : LO + N5] = new
            return carry

        lax.fori_loop(s, B + 2 * HZ - s, sub, 0)

    src = cb if NSUB % 2 == 0 else ca
    rflat = rr.reshape(B * B, X)

    def last(z, carry):
        at, up = slice(HY, HY + B), slice(4, 4 + B)
        new = ((k0[z, up] * src[z, at]
                + cym[z, up] * src[z, HY - 1 : HY - 1 + B])
               - (cyp[z, up] * src[z, HY + 1 : HY + 1 + B]
                  - czm[z, up] * src[z - 1, at])
               - czp[z, up] * src[z + 1, at])
        rflat[pl.ds(z - HZ, B, stride=B), :] = new
        return carry

    lax.fori_loop(HZ, HZ + B, last, 0)

    g0, gl = local_scan(rr, ay, by, ff, gg, iy)
    put_pair(gsy, 0, g0, gl)
    gry[g] = gsy[lax.rem(g, C)]
    for k in range(1, ny):
        to_y(gsy, gry, grsem.at[0], k).start()

    factor(kz, zfirst, zlast, az, bz, iz, lz, hz, tmp)
    edges[1].wait_recv()
    put_pair(psz, 0, lz[0] + 1.0 / (HALF_RATE * (kze[...] + kz[0])), hz[B - 1])
    put_pair(psz, 8, hz[0], hz[0])
    prz[p] = psz[lax.rem(p, C)]
    for k in range(1, nz):
        to_z(psz.at[:, 0:PR], prz.at[:, 0:PR], psem.at[1], k).start()

    wait_all(pry.at[:, 0:PR], ny - 1, psem.at[0, 1])
    owner_matrix(ny, pry, my, yy, rf, rb)

    wait_all(gry, ny - 1, grsem.at[0, 1])
    owner_scan(ny, gry, my, uy, vy)
    yc = lax.rem(g, C)
    yb = g - yc
    rety[yc] = owner_result(g, uy, vy, yy)
    for m in range(1, C):
        b = yb + lax.rem(yc + m, C)
        rsy[m] = owner_result(b, uy, vy, yy)
        pltpu.make_async_remote_copy(
            rsy.at[m], rety.at[yc], rtsem.at[0, 0], rtsem.at[0, 1],
            device_id=(p, b), device_id_type=MESH).start()

    def base(j, carry):
        ff[j] = (ff[j] + gg[j]) * iy[j]
        return carry

    lax.fori_loop(0, B, base, 0)

    wait_all(rety, C - 1, rtsem.at[0, 1])
    flo, fhi = get_pair(rety)
    uflat = uz.reshape(B * B, X)

    def end_y(j, carry):
        uflat[pl.ds(j, B, stride=B), :] = ff[j] + flo * ly[j] + fhi * hy[j]
        return carry

    lax.fori_loop(0, B, end_y, 0)

    g0, gl = local_scan(uz, az, bz, ff, gg, iz)
    put_pair(gsz, 0, g0, gl)
    grz[p] = gsz[lax.rem(p, C)]
    for k in range(1, nz):
        to_z(gsz, grz, grsem.at[1], k).start()

    def base_z(j, carry):
        ff[j] = (ff[j] + gg[j]) * iz[j]
        return carry

    lax.fori_loop(0, B, base_z, 0)
    wait_all(prz.at[:, 0:PR], nz - 1, psem.at[1, 1])
    owner_matrix(nz, prz, mz, yz, rf, rb)

    wait_all(grz, nz - 1, grsem.at[1, 1])
    owner_scan(nz, grz, mz, uo, vo)
    zc = lax.rem(p, C)
    retz[zc] = owner_result(p, uo, vo, yz)
    others = [o for o in range(-(C // 2), C // 2) if o != 0]
    for m, o in enumerate(others):
        b = zi(o)
        rsz[m] = owner_result(b, uo, vo, yz)
        pltpu.make_async_remote_copy(
            rsz.at[m], retz.at[zc], rtsem.at[1, 0], rtsem.at[1, 1],
            device_id=(b, g), device_id_type=MESH).start()
    wait_all(retz, C - 1, rtsem.at[1, 1])
    flo, fhi = get_pair(retz)

    def end_z(j, carry):
        out[j] = ff[j] + flo * lz[j] + fhi * hz[j]
        return carry

    stores = []
    for j in range(0, B, OUT):
        lax.fori_loop(j, j + OUT, end_z, 0)
        st = pltpu.make_async_copy(
            out.at[j : j + OUT], o_hbm.at[j : j + OUT], lsem.at[4 + j // OUT])
        st.start()
        stores.append(st)
    for h in edges + halo:
        h.wait_send()
    wait_all(pry.at[:, 0:PR], ny - 1, psem.at[0, 0])
    wait_all(prz.at[:, 0:PR], nz - 1, psem.at[1, 0])
    wait_all(gry, ny - 1, grsem.at[0, 0])
    wait_all(grz, nz - 1, grsem.at[1, 0])
    wait_all(rety, C - 1, rtsem.at[0, 0])
    wait_all(retz, C - 1, rtsem.at[1, 0])
    for st in stores:
        st.wait()


def local(nz, ny, tracer, y_speed, z_speed, kappa):
    f32 = jnp.float32
    pad = pltpu.VMEM((B + 2 * HZ, B + 2 * HY, X), f32)
    blk = pltpu.VMEM((B, B, X), f32)
    wgt = pltpu.VMEM((B + 2 * HZ, B + 8, X), f32)

    def tiles(n, rows=8):
        return pltpu.VMEM((n, rows, X), f32)

    scratch = (
        [pad] * 4 + [blk] * 2 + [wgt] * 5
        + [blk] * 5 + [blk] * 5 + [blk] * 6
        + [tiles(C, 16), tiles(C, 16), tiles(ny, 16), tiles(nz, 16)]
        + [tiles(C), tiles(C), tiles(ny), tiles(nz)]
        + [tiles(ny), tiles(ny + 1), tiles(ny + 1), tiles(ny + 1)]
        + [tiles(nz), tiles(nz + 1), tiles(nz + 1), tiles(nz + 1)]
        + [tiles(ny), tiles(ny)]
        + [tiles(C), tiles(C), tiles(C), tiles(C)]
        + [tiles(B), pltpu.VMEM((B, X), f32), pltpu.SemaphoreType.DMA((4 + B // OUT,)), pltpu.SemaphoreType.DMA((24,)),
           pltpu.SemaphoreType.DMA((24,)), pltpu.SemaphoreType.DMA((2, 2)),
           pltpu.SemaphoreType.DMA((2, 2)), pltpu.SemaphoreType.DMA((2, 2)),
           pltpu.SemaphoreType.DMA((4,)),
           pltpu.SemaphoreType.REGULAR((4,)), pltpu.SemaphoreType.REGULAR((4,))]
    )
    return pl.pallas_call(
        functools.partial(kernel, nz, ny),
        out_shape=jax.ShapeDtypeStruct(tracer.shape, f32),
        in_specs=[pl.BlockSpec(memory_space=pl.ANY)] * 4,
        out_specs=pl.BlockSpec(memory_space=pl.ANY),
        scratch_shapes=scratch,
        compiler_params=pltpu.CompilerParams(
            collective_id=0, has_side_effects=True, vmem_limit_bytes=56000000),
    )(tracer, y_speed, z_speed, kappa)


def solution(mesh):
    nz, ny = mesh.shape["gz"], mesh.shape["gy"]
    return jax.shard_map(
        functools.partial(local, nz, ny),
        mesh=mesh,
        in_specs=(P("gz", "gy", None),) * 4,
        out_specs=P("gz", "gy", None),
        check_vma=False,
    )
```

```python
import functools

import jax
import jax.numpy as jnp
from jax import lax
from jax.experimental import pallas as pl
from jax.experimental.pallas import tpu as pltpu
from jax.sharding import PartitionSpec as P

NSUB = 4
RATE = 500.0
HALF_RATE = 250.0
B = 32
X = 128
HZ = 4
HY = 8
C = 8
PR = 12
OUT = 8
MESH = pl.DeviceIdType.MESH


def low_rows():
    return lax.broadcasted_iota(jnp.int32, (8, X), 0) < 4


def swap(t):
    return pltpu.roll(t, 4, 0)


def factor(kap, first, last, a_ref, b_ref, inv_ref, lo_ref, hi_ref, tmp_ref):
    e0 = 1.0 + first * kap[0]
    b0 = 1.0 + last * kap[B - 1]
    one = jnp.ones_like(e0)
    inv_ref[0] = e0
    lo_ref[0] = one
    tmp_ref[B - 1] = b0
    hi_ref[B - 1] = one

    def step(s, carry):
        e, eb, ac, bc, kf, kb = carry
        t = B - 1 - s
        kn = kap[s]
        kp = kap[t]
        face = HALF_RATE * (kf + kn)
        a = face / (e + face)
        e = 1.0 + a * e
        ac = ac * a
        faceb = HALF_RATE * (kb + kp)
        b = faceb / (eb + faceb)
        eb = 1.0 + b * eb
        bc = bc * b
        a_ref[s] = a
        inv_ref[s] = e
        lo_ref[s] = ac
        b_ref[t] = b
        tmp_ref[t] = eb
        hi_ref[t] = bc
        return e, eb, ac, bc, kn, kp

    lax.fori_loop(1, B, step, (e0, b0, one, one, kap[0], kap[B - 1]))

    def finish(j, carry):
        inv = 1.0 / (inv_ref[j] + tmp_ref[j] - 1.0)
        inv_ref[j] = inv
        lo_ref[j] = lo_ref[j] * inv
        hi_ref[j] = hi_ref[j] * inv
        return carry

    lax.fori_loop(0, B, finish, 0)


def put_pair(dst, row, first, second):
    low = low_rows()
    for q in range(4):
        f = first[8 * q : 8 * q + 8]
        s = second[8 * q : 8 * q + 8]
        dst[2 * q, row : row + 8] = jnp.where(low, f, swap(s))
        dst[2 * q + 1, row : row + 8] = jnp.where(low, swap(f), s)


def get_pair(src):
    low = low_rows()
    first, second = [], []
    for q in range(4):
        t0 = src[2 * q]
        t1 = src[2 * q + 1]
        first.append(jnp.where(low, t0, swap(t1)))
        second.append(jnp.where(low, swap(t0), t1))
    return jnp.concatenate(first, axis=0), jnp.concatenate(second, axis=0)


def owner_matrix(n, prm, m_ref, y_ref, rf_ref, rb_ref):
    low = low_rows()
    zero = jnp.zeros((8, X), jnp.float32)

    def block(i):
        c = prm[i, 8:16]
        return prm[i, 0:8], jnp.where(low, c, swap(c))

    y_ref[0] = zero
    y_ref[n] = zero
    r0 = prm[0, 0:8]
    rb0 = prm[n - 1, 0:8]
    rf_ref[0] = r0
    rb_ref[n - 1] = rb0
    m_ref[0] = zero
    m_ref[n - 1] = zero

    def step(s, carry):
        r, rb = carry
        z, zt = block(s)
        t = zt / (r + swap(z))
        r = z - zt * t
        rf_ref[s] = r
        i = n - 1 - s
        zb, ztb = block(i)
        tb = ztb / (rb + swap(zb))
        rb = zb - ztb * tb
        rb_ref[i] = rb
        m_ref[s] = jnp.where(low, m_ref[s], t)
        m_ref[i] = jnp.where(low, tb, m_ref[i])
        return r, rb

    def clear(s, carry):
        m_ref[s] = zero
        return carry

    lax.fori_loop(0, n, clear, 0)
    lax.fori_loop(1, n, step, (r0, rb0))

    def admit(i, carry):
        y_ref[i] = 1.0 / (swap(rf_ref[i - 1]) + rb_ref[i])
        return carry

    lax.fori_loop(1, n, admit, 0)


def owner_scan(n, g_ref, m_ref, u_ref, v_ref):
    zero = jnp.zeros((8, X), jnp.float32)
    u_ref[0] = zero
    v_ref[n] = zero

    def step(s, carry):
        u, v = carry
        g = g_ref[s]
        m = m_ref[s]
        u = g - m * swap(g) + m * u
        u_ref[s + 1] = u
        i = n - 1 - s
        gb = g_ref[i]
        mb = m_ref[i]
        v = gb - mb * swap(gb) + mb * v
        v_ref[i] = v
        return u, v

    lax.fori_loop(0, n, step, (zero, zero))


def owner_result(b, u_ref, v_ref, y_ref):
    low = low_rows()
    here = (swap(u_ref[b]) - v_ref[b]) * y_ref[b]
    after = (swap(u_ref[b + 1]) - v_ref[b + 1]) * y_ref[b + 1]
    return jnp.where(low, here, -swap(after))


def local_scan(r_ref, a_ref, b_ref, f_ref, g_ref, inv_ref):
    r0 = r_ref[0]
    rb0 = r_ref[B - 1]
    f_ref[0] = r0
    g_ref[B - 1] = jnp.zeros_like(r0)

    def step(s, carry):
        f, g = carry
        t = B - 1 - s
        f = r_ref[s] + a_ref[s] * f
        bg = b_ref[t] * g
        g = r_ref[t] + bg
        f_ref[s] = f
        g_ref[t] = bg
        return f, g

    f, g = lax.fori_loop(1, B, step, (r0, rb0))
    return g * inv_ref[0], f * inv_ref[B - 1]


def kernel(nz, ny, *refs):
    (c_hbm, v_hbm, w_hbm, k_hbm, o_hbm,
     ca, cb, vv, ww, kz, ky, k0, cym, cyp, czm, czp,
     ay, by, iy, ly, hy, az, bz, iz, lz, hz, tmp, rr, ff, gg, uz, out,
     psy, psz, pry, prz, gsy, gsz, gry, grz,
     my, yy, uy, vy, mz, yz, uo, vo, rf, rb,
     rsy, rsz, rety, retz,
     kye, kze, lsem, hsend, hrecv, psem, grsem, rtsem, ksem, ysem, zsem) = refs
    p = lax.axis_index("gz")
    g = lax.axis_index("gy")

    def zi(k):
        return lax.rem(p + k + nz, nz)

    def yi(k):
        return lax.rem(g + k + ny, ny)

    bar = pltpu.get_barrier_semaphore()
    neighbours = [(dz, dy) for dz in (1, 0, -1) for dy in (1, 0, -1) if dz or dy]
    for dz, dy in neighbours:
        pl.semaphore_signal(bar, inc=1, device_id=(zi(dz), yi(dy)), device_id_type=MESH)

    def greet(r):
        d = 1 << r
        if 2 * d < ny:
            for k in (d, -d):
                pl.semaphore_signal(ysem.at[r], inc=1, device_id=(p, yi(k)), device_id_type=MESH)
        if 2 * d < nz:
            for k in (d, -d):
                pl.semaphore_signal(zsem.at[r], inc=1, device_id=(zi(k), g), device_id_type=MESH)

    def greeted(r):
        if 2 << r < ny:
            pl.semaphore_wait(ysem.at[r], 2)
        if 2 << r < nz:
            pl.semaphore_wait(zsem.at[r], 2)

    loads = [
        pltpu.make_async_copy(k_hbm, kz, lsem.at[0]),
        pltpu.make_async_copy(c_hbm, ca.at[HZ : HZ + B, HY : HY + B], lsem.at[1]),
        pltpu.make_async_copy(v_hbm, vv.at[HZ : HZ + B, HY : HY + B], lsem.at[2]),
        pltpu.make_async_copy(w_hbm, ww.at[HZ : HZ + B, HY : HY + B], lsem.at[3]),
    ]
    for ld in loads:
        ld.start()

    pl.semaphore_wait(bar, len(neighbours))

    def near(d, size, pad, width):
        if d == 0:
            return slice(0, size), slice(pad, pad + size)
        if d > 0:
            return slice(size - width, size), slice(pad - width, pad)
        return slice(0, width), slice(pad + size, pad + size + width)

    halo = []
    for dz, dy in ((0, 1), (0, -1), (1, 0), (-1, 0), (1, 1), (1, -1), (-1, 1), (-1, -1)):
        for src, dst, wz, wy in ((c_hbm, ca, 4, 4), (v_hbm, vv, 3, 4), (w_hbm, ww, 4, 3)):
            if dz and dy:
                wz, wy = 3, 3
            zs, zd = near(dz, B, HZ, wz)
            ys, yd = near(dy, B, HY, wy)
            i = len(halo)
            halo.append(pltpu.make_async_remote_copy(
                src.at[zs, ys], dst.at[zd, yd], hsend.at[i], hrecv.at[i],
                device_id=(zi(dz), yi(dy)), device_id_type=MESH))
    edges = [
        pltpu.make_async_remote_copy(
            k_hbm.at[:, B - 1 : B], kye.at[:, 0:1], ksem.at[0], ksem.at[1],
            device_id=(p, yi(1)), device_id_type=MESH),
        pltpu.make_async_remote_copy(
            k_hbm.at[B - 1], kze, ksem.at[2], ksem.at[3],
            device_id=(zi(1), g), device_id_type=MESH),
    ]
    for h in edges + halo:
        h.start()
    greet(0)

    loads[0].wait()
    kflat = kz.reshape(B * B, X)

    def turn(j, carry):
        ky[j] = kflat[pl.ds(j, B, stride=B), :]
        return carry

    lax.fori_loop(0, B, turn, 0)
    yfirst = jnp.where(g == 0, RATE, 0.0).astype(jnp.float32)
    ylast = jnp.where(g == ny - 1, RATE, 0.0).astype(jnp.float32)
    zfirst = jnp.where(p == 0, RATE, 0.0).astype(jnp.float32)
    zlast = jnp.where(p == nz - 1, RATE, 0.0).astype(jnp.float32)

    greeted(0)
    greet(1)
    factor(ky, yfirst, ylast, ay, by, iy, ly, hy, tmp)
    greeted(1)
    greet(2)
    edges[0].wait_recv()
    below = kye.reshape(B * 8, X)[pl.ds(0, B, stride=8), :]
    put_pair(psy, 0, ly[0] + 1.0 / (HALF_RATE * (below + ky[0])), hy[B - 1])
    put_pair(psy, 8, hy[0], hy[0])
    pry[g] = psy[lax.rem(g, C)]

    def to_y(src, dst, sem, k):
        return pltpu.make_async_remote_copy(
            src.at[lax.rem(g + k, C)], dst.at[g], sem.at[0], sem.at[1],
            device_id=(p, yi(k)), device_id_type=MESH)

    def to_z(src, dst, sem, k):
        return pltpu.make_async_remote_copy(
            src.at[lax.rem(p + k, C)], dst.at[p], sem.at[0], sem.at[1],
            device_id=(zi(k), g), device_id_type=MESH)

    def wait_all(ref, count, sem):
        part = ref.at[pl.ds(0, count)]
        pltpu.make_async_copy(part, part, sem).wait()

    greeted(2)
    greet(3)
    greeted(3)


    for ld in loads[1:]:
        ld.wait()
    for h in halo:
        h.wait_recv()
    for k in range(1, ny):
        to_y(psy.at[:, 0:PR], pry.at[:, 0:PR], psem.at[0], k).start()

    zero3 = jnp.zeros((HZ, B + 2 * HY, X), jnp.float32)
    zero_row = jnp.zeros((HY, X), jnp.float32)

    def zero_y(at):
        def body(z, carry):
            for ref in (ca, vv, ww):
                ref[z, at : at + HY] = zero_row
            return carry

        lax.fori_loop(0, B + 2 * HZ, body, 0)

    @pl.when(p == 0)
    def _():
        for ref in (ca, vv, ww):
            ref[0:HZ] = zero3

    @pl.when(p == nz - 1)
    def _():
        for ref in (ca, vv, ww):
            ref[HZ + B : 2 * HZ + B] = zero3

    @pl.when(g == 0)
    def _():
        zero_y(0)

    @pl.when(g == ny - 1)
    def _():
        zero_y(HY + B)

    LO, N5 = 4, B + 8

    def z_face(a, b):
        f = 0.5 * (a + b)
        return jnp.maximum(f, 0.0), jnp.minimum(f, 0.0)

    def weights(z, carry):
        wc, zm_pos, zm_neg = carry
        wp = ww[z + 1, LO : LO + N5]
        zp_pos, zp_neg = z_face(wc, wp)
        vc = vv[z, LO : LO + N5]
        ym_pos, ym_neg = z_face(vv[z, LO - 1 : LO - 1 + N5], vc)
        yp_pos, yp_neg = z_face(vc, vv[z, LO + 1 : LO + 1 + N5])
        cyp[z] = yp_neg
        cym[z] = ym_pos
        czp[z] = zp_neg
        czm[z] = zm_pos
        k0[z] = ((1.0 - yp_pos) + (ym_neg - zp_pos)) + zm_neg
        return wp, zp_pos, zp_neg

    w1 = ww[1, LO : LO + N5]
    lax.fori_loop(1, B + 2 * HZ - 1, weights, (w1, *z_face(ww[0, LO : LO + N5], w1)), unroll=2)

    wrefs = (k0, cym, cyp, czm, czp)
    zero_w = jnp.zeros((HZ - 1, N5, X), jnp.float32)

    def zero_wy(at):
        def body(z, carry):
            for ref in wrefs:
                ref[z, at : at + 4] = jnp.zeros((4, X), jnp.float32)
            return carry

        lax.fori_loop(1, B + 2 * HZ - 1, body, 0)

    @pl.when(p == 0)
    def _():
        for ref in wrefs:
            ref[1:HZ] = zero_w

    @pl.when(p == nz - 1)
    def _():
        for ref in wrefs:
            ref[HZ + B : 2 * HZ + B - 1] = zero_w

    @pl.when(g == 0)
    def _():
        zero_wy(0)

    @pl.when(g == ny - 1)
    def _():
        zero_wy(4 + B)

    for s in range(1, NSUB):
        src, dst = (ca, cb) if s % 2 == 1 else (cb, ca)

        def sub(z, carry, src=src, dst=dst):
            new = ((k0[z] * src[z, LO : LO + N5]
                    + cym[z] * src[z, LO - 1 : LO - 1 + N5])
                   - (cyp[z] * src[z, LO + 1 : LO + 1 + N5]
                      - czm[z] * src[z - 1, LO : LO + N5])
                   - czp[z] * src[z + 1, LO : LO + N5])
            dst[z, LO : LO + N5] = new
            return carry

        lax.fori_loop(s, B + 2 * HZ - s, sub, 0)

    src = cb if NSUB % 2 == 0 else ca
    rflat = rr.reshape(B * B, X)

    def last(z, carry):
        at, up = slice(HY, HY + B), slice(4, 4 + B)
        new = ((k0[z, up] * src[z, at]
                + cym[z, up] * src[z, HY - 1 : HY - 1 + B])
               - (cyp[z, up] * src[z, HY + 1 : HY + 1 + B]
                  - czm[z, up] * src[z - 1, at])
               - czp[z, up] * src[z + 1, at])
        rflat[pl.ds(z - HZ, B, stride=B), :] = new
        return carry

    lax.fori_loop(HZ, HZ + B, last, 0)

    g0, gl = local_scan(rr, ay, by, ff, gg, iy)
    put_pair(gsy, 0, g0, gl)
    gry[g] = gsy[lax.rem(g, C)]
    for k in range(1, ny):
        to_y(gsy, gry, grsem.at[0], k).start()

    factor(kz, zfirst, zlast, az, bz, iz, lz, hz, tmp)
    edges[1].wait_recv()
    put_pair(psz, 0, lz[0] + 1.0 / (HALF_RATE * (kze[...] + kz[0])), hz[B - 1])
    put_pair(psz, 8, hz[0], hz[0])
    prz[p] = psz[lax.rem(p, C)]
    for k in range(1, nz):
        to_z(psz.at[:, 0:PR], prz.at[:, 0:PR], psem.at[1], k).start()

    wait_all(pry.at[:, 0:PR], ny - 1, psem.at[0, 1])
    owner_matrix(ny, pry, my, yy, rf, rb)

    wait_all(gry, ny - 1, grsem.at[0, 1])
    owner_scan(ny, gry, my, uy, vy)
    yc = lax.rem(g, C)
    yb = g - yc
    rety[yc] = owner_result(g, uy, vy, yy)
    for m in range(1, C):
        b = yb + lax.rem(yc + m, C)
        rsy[m] = owner_result(b, uy, vy, yy)
        pltpu.make_async_remote_copy(
            rsy.at[m], rety.at[yc], rtsem.at[0, 0], rtsem.at[0, 1],
            device_id=(p, b), device_id_type=MESH).start()

    def base(j, carry):
        ff[j] = (ff[j] + gg[j]) * iy[j]
        return carry

    lax.fori_loop(0, B, base, 0)

    wait_all(rety, C - 1, rtsem.at[0, 1])
    flo, fhi = get_pair(rety)
    uflat = uz.reshape(B * B, X)

    def end_y(j, carry):
        uflat[pl.ds(j, B, stride=B), :] = ff[j] + flo * ly[j] + fhi * hy[j]
        return carry

    lax.fori_loop(0, B, end_y, 0)

    g0, gl = local_scan(uz, az, bz, ff, gg, iz)
    put_pair(gsz, 0, g0, gl)
    grz[p] = gsz[lax.rem(p, C)]
    for k in range(1, nz):
        to_z(gsz, grz, grsem.at[1], k).start()

    def base_z(j, carry):
        ff[j] = (ff[j] + gg[j]) * iz[j]
        return carry

    lax.fori_loop(0, B, base_z, 0)
    wait_all(prz.at[:, 0:PR], nz - 1, psem.at[1, 1])
    owner_matrix(nz, prz, mz, yz, rf, rb)

    wait_all(grz, nz - 1, grsem.at[1, 1])
    owner_scan(nz, grz, mz, uo, vo)
    zc = lax.rem(p, C)
    retz[zc] = owner_result(p, uo, vo, yz)
    others = [o for o in range(-(C // 2), C // 2) if o != 0]
    for m, o in enumerate(others):
        b = zi(o)
        rsz[m] = owner_result(b, uo, vo, yz)
        pltpu.make_async_remote_copy(
            rsz.at[m], retz.at[zc], rtsem.at[1, 0], rtsem.at[1, 1],
            device_id=(b, g), device_id_type=MESH).start()
    wait_all(retz, C - 1, rtsem.at[1, 1])
    flo, fhi = get_pair(retz)

    def end_z(j, carry):
        out[j] = ff[j] + flo * lz[j] + fhi * hz[j]
        return carry

    stores = []
    for j in range(0, B, OUT):
        lax.fori_loop(j, j + OUT, end_z, 0)
        st = pltpu.make_async_copy(
            out.at[j : j + OUT], o_hbm.at[j : j + OUT], lsem.at[4 + j // OUT])
        st.start()
        stores.append(st)
    for h in edges + halo:
        h.wait_send()
    wait_all(pry.at[:, 0:PR], ny - 1, psem.at[0, 0])
    wait_all(prz.at[:, 0:PR], nz - 1, psem.at[1, 0])
    wait_all(gry, ny - 1, grsem.at[0, 0])
    wait_all(grz, nz - 1, grsem.at[1, 0])
    wait_all(rety, C - 1, rtsem.at[0, 0])
    wait_all(retz, C - 1, rtsem.at[1, 0])
    for st in stores:
        st.wait()


def local(nz, ny, tracer, y_speed, z_speed, kappa):
    f32 = jnp.float32
    pad = pltpu.VMEM((B + 2 * HZ, B + 2 * HY, X), f32)
    blk = pltpu.VMEM((B, B, X), f32)
    wgt = pltpu.VMEM((B + 2 * HZ, B + 8, X), f32)

    def tiles(n, rows=8):
        return pltpu.VMEM((n, rows, X), f32)

    scratch = (
        [pad] * 4 + [blk] * 2 + [wgt] * 5
        + [blk] * 5 + [blk] * 5 + [blk] * 6
        + [tiles(C, 16), tiles(C, 16), tiles(ny, 16), tiles(nz, 16)]
        + [tiles(C), tiles(C), tiles(ny), tiles(nz)]
        + [tiles(ny), tiles(ny + 1), tiles(ny + 1), tiles(ny + 1)]
        + [tiles(nz), tiles(nz + 1), tiles(nz + 1), tiles(nz + 1)]
        + [tiles(ny), tiles(ny)]
        + [tiles(C), tiles(C), tiles(C), tiles(C)]
        + [tiles(B), pltpu.VMEM((B, X), f32), pltpu.SemaphoreType.DMA((4 + B // OUT,)), pltpu.SemaphoreType.DMA((24,)),
           pltpu.SemaphoreType.DMA((24,)), pltpu.SemaphoreType.DMA((2, 2)),
           pltpu.SemaphoreType.DMA((2, 2)), pltpu.SemaphoreType.DMA((2, 2)),
           pltpu.SemaphoreType.DMA((4,)),
           pltpu.SemaphoreType.REGULAR((4,)), pltpu.SemaphoreType.REGULAR((4,))]
    )
    return pl.pallas_call(
        functools.partial(kernel, nz, ny),
        out_shape=jax.ShapeDtypeStruct(tracer.shape, f32),
        in_specs=[pl.BlockSpec(memory_space=pl.ANY)] * 4,
        out_specs=pl.BlockSpec(memory_space=pl.ANY),
        scratch_shapes=scratch,
        compiler_params=pltpu.CompilerParams(
            collective_id=0, has_side_effects=True, vmem_limit_bytes=56000000),
    )(tracer, y_speed, z_speed, kappa)


def solution(mesh):
    nz, ny = mesh.shape["gz"], mesh.shape["gy"]
    return jax.shard_map(
        functools.partial(local, nz, ny),
        mesh=mesh,
        in_specs=(P("gz", "gy", None),) * 4,
        out_specs=P("gz", "gy", None),
        check_vma=False,
    )
```
